128 devices in a mesh: dp: 4 (over y_hi, core), ctx: 32 (over x, y_lo, z).
Axes of the slice: x: 4, y: 4 (y_hi: 2, y_lo: 2; y = y_hi * 2 + y_lo), z: 4, core: 2. Of those that a mesh axis runs over, the one named last changes fastest.
Arguments:
- queries: bfloat16 [16384, 2048], P(('dp', 'ctx')), parts along dimension 0, may hold values from -9 to 9
- keys: bfloat16 [16384, 512], P(('dp', 'ctx')), parts along dimension 0, may hold values from -9 to 9
- values: bfloat16 [16384, 512], P(('dp', 'ctx')), parts along dimension 0, may hold values from -6 to 6
- grad_out: bfloat16 [16384, 2048], P(('dp', 'ctx')), parts along dimension 0, may hold values from -6 to 6
- positions: int32 [1024], P('dp'), parts along dimension 0, may hold values from 0 to 4095, as said below
Outputs:
- attended: bfloat16 [16384, 2048], P(('dp', 'ctx')), parts along dimension 0
- grad_queries: bfloat16 [16384, 2048], P(('dp', 'ctx')), parts along dimension 0
- grad_keys: bfloat16 [16384, 512], P(('dp', 'ctx')), parts along dimension 0
- grad_values: bfloat16 [16384, 512], P(('dp', 'ctx')), parts along dimension 0
The draws below stay inside these ranges and needn't reach their ends.
There are 4 independent parts, one for each index of `dp`. The reference program is written for one: setup_inputs(seed, part) draws one part's arguments, and reference() takes and returns one part's arrays. A program takes and returns all parts, laid end to end along the dimension named above; each array names one. Nothing has to cross between parts.
Inputs may be any that keep to these rules, and one draw needn't show every extreme that they name: 256 distinct token positions in increasing order; the 128 tokens of one index of ctx hold at most 32 of them, and one index holds exactly 32.
All inputs are finite; a program needn't handle non-finite values.
Results may differ from the reference program's by a relative error of at most 0.0075.
Values may be sent and summed in bfloat16 or wider, within the bound.
No kernel may reach another device: no remote copies, remote signals or barrier semaphores. Data moves between devices by JAX's collectives and lax.ppermute only.
A program may use at most 192 MiB of HBM per device.

```python
import math
import jax
import jax.numpy as jnp
from jax import lax

HQ = 16
HK = 4
DH = 128
BLOCK = 64
GLOB = 256
CAP = 32
TOK_DEV = 128
SEQ = 4096


def global_positions(key):
    baseline_value = jax.random.fold_in(key, 11)
    heavy_random_key, boost_random_key, jitter_random_key, shift_random_key = jax.random.split(baseline_value, 4)
    shard_pieces = SEQ // TOK_DEV
    heavy = jax.random.randint(heavy_random_key, (), 0, shard_pieces)
    extra_boost = jax.random.randint(boost_random_key, (shard_pieces,), 0, 2)
    random_jitter = jax.random.randint(jitter_random_key, (shard_pieces, CAP), 0, 1 << 14)
    shard_ids = jnp.arange(shard_pieces)[:, None]
    score_logit = random_jitter + extra_boost[:, None] * (1 << 13)
    score_logit = jnp.where(shard_ids == heavy, 1 << 16, score_logit)
    distinct = score_logit * (shard_pieces * CAP) + jnp.arange(shard_pieces * CAP).reshape(shard_pieces, CAP)
    unused, chosen = lax.top_k(distinct.reshape(-1), GLOB)
    picked = jnp.zeros((shard_pieces * CAP,), jnp.int32).at[chosen].set(1)
    offsets = jax.vmap(lambda one_key: jnp.sort(jax.random.permutation(one_key, TOK_DEV)[:CAP]))(jax.random.split(shift_random_key, shard_pieces))
    spots = (shard_ids * TOK_DEV + offsets).reshape(-1)
    ranked = jnp.where(picked == 1, spots, spots + SEQ)
    return jnp.sort(ranked)[:GLOB].astype(jnp.int32)


def draw_positions(key, part):
    return global_positions(key)


def draw_queries(key, part):
    inner = jax.random.fold_in(key, 31)
    drawn = jnp.clip(1.5 * jax.random.normal(inner, (SEQ, HQ * DH), jnp.float32), -9.0, 9.0)
    return drawn.astype(jnp.bfloat16)


def draw_keys(key, part):
    inner = jax.random.fold_in(key, 37)
    drawn = jnp.clip(1.5 * jax.random.normal(inner, (SEQ, HK * DH), jnp.float32), -9.0, 9.0)
    return drawn.astype(jnp.bfloat16)


def shard_levels(stream_key, shape, cuts, low, top_value):
    def one(position, blocks):
        draws = jax.random.uniform(jax.random.fold_in(jax.random.fold_in(stream_key, 6), position), (blocks,), jnp.float32, low / len(cuts), top_value / len(cuts))
        return jnp.repeat(jnp.exp(draws), shape[position] // blocks).reshape((-1,) + (1,) * (len(shape) - position - 1))

    loudness = one(*cuts[0])
    for cut in cuts[1:]:
        loudness = loudness * one(*cut)
    return loudness


def gaussian(key, extent, width, reach, cuts=(), dtype=jnp.bfloat16):
    level = shard_levels(key, extent, cuts, -0.22, 0.18) if cuts else 1.0
    array = jax.random.normal(key, extent, jnp.float32) * width * level
    return jnp.minimum(jnp.maximum(array, -reach), reach).astype(dtype)


def setup_inputs(seed: int = 0, part: int = 0) -> dict:
    streams_of = jax.random.split(jax.random.key(seed), 6)
    part_splits = jax.random.split(jax.random.fold_in(streams_of[5], part), 6)
    queries = draw_queries(jax.random.fold_in(jax.random.fold_in(streams_of[5], part), 71), part)
    keys = draw_keys(jax.random.fold_in(jax.random.fold_in(streams_of[5], part), 71), part)
    values = gaussian(part_splits[2], (SEQ, HK * DH), 1.0, 6.0, ((0, 32),))
    grad_out = gaussian(part_splits[3], (SEQ, HQ * DH), 1.0, 6.0, ((0, 32),))
    positions = draw_positions(jax.random.fold_in(jax.random.fold_in(streams_of[5], part), 71), part)
    return {"queries": queries, "keys": keys, "values": values, "grad_out": grad_out, "positions": positions}


highest = lax.Precision.HIGHEST

def rounded(source):
    return lax.optimization_barrier(source.astype(jnp.bfloat16)).astype(jnp.float32)

def window_group(pieces, glob_keys, glob_values, score_scale):
    query_block, grad_block, key_window, value_window, key_usable, query_live = pieces
    near = jnp.einsum('bqard,bkad->barqk', query_block, key_window, precision=highest) * score_scale
    far = jnp.einsum('bqard,gad->barqg', query_block, glob_keys, precision=highest) * score_scale
    near = jnp.where(key_usable[:, None, None, None, :], near, -jnp.inf)
    row_top = jnp.maximum(lax.optimization_barrier(jnp.max(near, axis=-1)), lax.optimization_barrier(jnp.max(far, axis=-1)))
    near_weight = jnp.exp(near - row_top[..., None])
    far_weight = jnp.exp(far - row_top[..., None])
    total = lax.optimization_barrier(jnp.sum(near_weight, axis=-1)) + lax.optimization_barrier(jnp.sum(far_weight, axis=-1))
    mixed = jnp.einsum('barqk,bkad->bqard', rounded(near_weight), value_window, precision=highest)
    mixed = mixed + jnp.einsum('barqg,gad->bqard', rounded(far_weight), glob_values, precision=highest)
    attended = mixed / jnp.transpose(total, (0, 3, 1, 2))[..., None]
    delta = jnp.transpose(lax.optimization_barrier(jnp.sum(grad_block * attended, axis=-1)), (0, 2, 3, 1))
    live = query_live[:, None, None, :, None]
    near_prob = near_weight / total[..., None]
    far_prob = far_weight / total[..., None]
    near_dprob = jnp.einsum('bqard,bkad->barqk', grad_block, value_window, precision=highest)
    far_dprob = jnp.einsum('bqard,gad->barqg', grad_block, glob_values, precision=highest)
    near_dscore = rounded(near_prob * (near_dprob - delta[..., None]) * live)
    far_dscore = rounded(far_prob * (far_dprob - delta[..., None]) * live)
    near_round = rounded(near_prob * live)
    far_round = rounded(far_prob * live)
    grad_query = jnp.einsum('barqk,bkad->bqard', near_dscore, key_window, precision=highest)
    grad_query = score_scale * (grad_query + jnp.einsum('barqg,gad->bqard', far_dscore, glob_keys, precision=highest))
    grad_key_win = score_scale * jnp.einsum('barqk,bqard->bkad', near_dscore, query_block, precision=highest)
    grad_value_win = jnp.einsum('barqk,bqard->bkad', near_round, grad_block, precision=highest)
    grad_key_glob = score_scale * jnp.einsum('barqg,bqard->gad', far_dscore, query_block, precision=highest)
    grad_value_glob = jnp.einsum('barqg,bqard->gad', far_round, grad_block, precision=highest)
    return (attended, grad_query, grad_key_win, grad_value_win, grad_key_glob, grad_value_glob)

def global_head(pieces, score_scale):
    query_head, grad_head, key_head, value_head = pieces
    score_logit = jnp.einsum('grd,ud->gru', query_head, key_head, precision=highest) * score_scale
    row_top = lax.optimization_barrier(jnp.max(score_logit, axis=-1))
    weight = jnp.exp(score_logit - row_top[..., None])
    total = lax.optimization_barrier(jnp.sum(weight, axis=-1))
    attended = jnp.einsum('gru,ud->grd', weight, value_head, precision=highest) / total[..., None]
    delta = lax.optimization_barrier(jnp.sum(grad_head * attended, axis=-1))
    prob = weight / total[..., None]
    dprob = jnp.einsum('grd,ud->gru', grad_head, value_head, precision=highest)
    dscore = rounded(prob * (dprob - delta[..., None]))
    prob_round = rounded(prob)
    grad_query = score_scale * jnp.einsum('gru,ud->grd', dscore, key_head, precision=highest)
    grad_key = score_scale * jnp.einsum('gru,grd->ud', dscore, query_head, precision=highest)
    grad_value = jnp.einsum('gru,grd->ud', prob_round, grad_head, precision=highest)
    return (attended, grad_query, grad_key, grad_value)

def spread_window(parts):
    empty_block = jnp.zeros((1,) + parts.shape[2:], jnp.float32)
    spread = jnp.concatenate([parts[:, 0], empty_block, empty_block], axis=0)
    spread = spread + jnp.concatenate([empty_block, parts[:, 1], empty_block], axis=0)
    spread = spread + jnp.concatenate([empty_block, empty_block, parts[:, 2]], axis=0)
    return spread[1:-1].reshape(SEQ, HK, DH)

def reference(queries, keys, values, grad_out, positions):
    q_per_kv = HQ // HK
    score_scale = 1.0 / math.sqrt(DH)
    blocks = SEQ // BLOCK
    query_all = queries.astype(jnp.float32).reshape(SEQ, HK, q_per_kv, DH)
    grad_all = grad_out.astype(jnp.float32).reshape(SEQ, HK, q_per_kv, DH)
    key_all = keys.astype(jnp.float32).reshape(SEQ, HK, DH)
    value_all = values.astype(jnp.float32).reshape(SEQ, HK, DH)
    is_global = jnp.zeros((SEQ,), jnp.int32).at[positions].set(1)
    padding = jnp.zeros((BLOCK, HK, DH), jnp.float32)
    key_ext = jnp.concatenate([padding, key_all, padding], axis=0).reshape(blocks + 2, BLOCK, HK, DH)
    value_ext = jnp.concatenate([padding, value_all, padding], axis=0).reshape(blocks + 2, BLOCK, HK, DH)
    key_window = jnp.concatenate([key_ext[:-2], key_ext[1:-1], key_ext[2:]], axis=1)
    value_window = jnp.concatenate([value_ext[:-2], value_ext[1:-1], value_ext[2:]], axis=1)
    border = jnp.ones((BLOCK,), jnp.int32)
    ext_usable = (jnp.concatenate([border, is_global, border]) == 0).reshape(blocks + 2, BLOCK)
    key_usable = jnp.concatenate([ext_usable[:-2], ext_usable[1:-1], ext_usable[2:]], axis=1)
    query_live = (1 - is_global).astype(jnp.float32).reshape(blocks, BLOCK)
    glob_keys = key_all[positions]
    glob_values = value_all[positions]
    per_step = 8
    step_count = blocks // per_step

    def regroup(source):
        return source.reshape((step_count, per_step) + source.shape[1:])
    stacked = (regroup(query_all.reshape(blocks, BLOCK, HK, q_per_kv, DH)), regroup(grad_all.reshape(blocks, BLOCK, HK, q_per_kv, DH)), regroup(key_window), regroup(value_window), regroup(key_usable), regroup(query_live))
    results = lax.map(lambda pieces: window_group(pieces, glob_keys, glob_values, score_scale), stacked)
    attended_loc = results[0].reshape(SEQ, HK, q_per_kv, DH)
    grad_query_loc = results[1].reshape(SEQ, HK, q_per_kv, DH)
    key_parts = results[2].reshape(blocks, 3, BLOCK, HK, DH)
    value_parts = results[3].reshape(blocks, 3, BLOCK, HK, DH)
    glob_key_grad = lax.optimization_barrier(jnp.sum(results[4], axis=0))
    glob_value_grad = lax.optimization_barrier(jnp.sum(results[5], axis=0))
    head_inputs = (jnp.transpose(query_all[positions], (1, 0, 2, 3)), jnp.transpose(grad_all[positions], (1, 0, 2, 3)), jnp.transpose(key_all, (1, 0, 2)), jnp.transpose(value_all, (1, 0, 2)))
    head_out = lax.map(lambda pieces: global_head(pieces, score_scale), head_inputs)
    attended = attended_loc.at[positions].set(jnp.transpose(head_out[0], (1, 0, 2, 3)))
    grad_query = grad_query_loc.at[positions].add(jnp.transpose(head_out[1], (1, 0, 2, 3)))
    grad_key = spread_window(key_parts).at[positions].add(glob_key_grad) + jnp.transpose(head_out[2], (1, 0, 2))
    grad_value = spread_window(value_parts).at[positions].add(glob_value_grad) + jnp.transpose(head_out[3], (1, 0, 2))
    return (attended.reshape(SEQ, HQ * DH).astype(jnp.bfloat16), grad_query.reshape(SEQ, HQ * DH).astype(jnp.bfloat16), grad_key.reshape(SEQ, HK * DH).astype(jnp.bfloat16), grad_value.reshape(SEQ, HK * DH).astype(jnp.bfloat16))
```

```python
import functools
import math

import jax
import jax.numpy as jnp
from jax import lax
from jax.experimental import pallas as pl
from jax.experimental.pallas import tpu as pltpu
from jax.sharding import PartitionSpec as P

HQ = 16
HK = 4
DH = 128
BLOCK = 64
REP = HQ // HK
GROUP = 4
CHUNK = 64
TILE = 512
ROWS = REP * BLOCK
SCALE = 1.0 / math.sqrt(DH)
EXP2 = SCALE * math.log2(math.e)
NEG = -1e30

F32 = jnp.float32
BF16 = jnp.bfloat16


def dot_nt(a, b):
    return lax.dot_general(a, b, (((1,), (1,)), ((), ())), preferred_element_type=F32)


def dot_nn(a, b):
    return lax.dot_general(a, b, (((1,), (0,)), ((), ())), preferred_element_type=F32)


def iota(shape, dim):
    return lax.broadcasted_iota(jnp.int32, shape, dim)


def prep_kernel(clusters, q_ref, k_ref, v_ref, g_ref, kv_ref, *qg_refs):
    z = lax.rem(lax.axis_index("ctx"), GROUP)
    wide = REP * DH
    for j in range(HK):
        one = jnp.concatenate(
            [k_ref[:, j * DH : (j + 1) * DH], v_ref[:, j * DH : (j + 1) * DH]], axis=1
        )
        for s in range(clusters):
            kv_ref[s * GROUP + j] = one
    for step in range(GROUP):
        col = pl.multiple_of(lax.rem(z + step, GROUP) * wide, wide)
        qg_refs[step][:, :wide] = q_ref[:, pl.ds(col, wide)]
        qg_refs[step][:, wide:] = g_ref[:, pl.ds(col, wide)]


def main_kernel(
    seq, toks, glob, bounds_ref, pos_ref, kv_hbm, *refs
):
    qg_in = refs[:GROUP]
    dkv_out = refs[GROUP]
    qg_out = refs[GROUP + 1 : 2 * GROUP + 1]
    (kvp, kvt, dkv, dkv_bf, qg, out, sc, dp, attg, kg, kgt, dkg, kv_sem, qg_sem, out_sem, dkv_sem) = refs[
        2 * GROUP + 1 :
    ]
    me = lax.axis_index("ctx")
    z = lax.rem(me, GROUP)
    ctoks = GROUP * toks
    wide = REP * DH
    tiles = seq // TILE
    first = (me // GROUP) * ctoks

    kv_copy = pltpu.make_async_copy(kv_hbm, kvp.at[pl.ds(BLOCK, seq)], kv_sem)
    kv_copy.start()
    qg_copies = []
    for step in range(GROUP):
        src = lax.rem(z + GROUP - step, GROUP)
        copy = pltpu.make_async_copy(
            qg_in[step], qg.at[pl.ds(pl.multiple_of(src * toks, toks), toks)], qg_sem.at[step]
        )
        copy.start()
        qg_copies.append(copy)

    kvp[0:BLOCK] = jnp.zeros((BLOCK, 2 * DH), BF16)
    kvp[BLOCK + seq : 2 * BLOCK + seq] = jnp.zeros((BLOCK, 2 * DH), BF16)
    dkv[...] = jnp.zeros_like(dkv)
    attg[...] = jnp.zeros_like(attg)
    dkg[...] = jnp.zeros_like(dkg)
    pos_row = pos_ref[...]
    eye = iota((glob, glob), 0) == iota((glob, glob), 1)
    pos_col = jnp.sum(
        jnp.where(eye, jnp.broadcast_to(pos_row, (glob, glob)), 0).astype(F32), axis=1, keepdims=True
    ).astype(jnp.int32)
    before = bounds_ref[0]
    count = bounds_ref[1] - before

    for copy in qg_copies:
        copy.wait()
    kv_copy.wait()

    def gather_tile(t, acc):
        off = pl.multiple_of(t * TILE, TILE)
        tile = kvp[pl.ds(pl.multiple_of(off + BLOCK, BLOCK), TILE), :]
        kvt[:, pl.ds(off, TILE)] = tile.T
        hot = (pos_col == off + iota((glob, TILE), 1)).astype(F32).astype(BF16)
        return acc + dot_nn(hot, tile)

    got = lax.fori_loop(0, tiles, gather_tile, jnp.zeros((glob, 2 * DH), F32)).astype(BF16)
    kg[...] = got
    kgt[...] = got.T

    tok_row = first + iota((1, ctoks), 1)
    is_row = jnp.sum((pos_col == tok_row).astype(F32), axis=0, keepdims=True)
    rank_row = jnp.sum((pos_col < tok_row).astype(F32), axis=0, keepdims=True)
    slot_row = jnp.where(is_row > 0.5, rank_row.astype(jnp.int32) - before, -1)

    def chunk(ch, carry):
        base = ch * CHUNK
        hot = (slot_row == base + iota((CHUNK, ctoks), 0)).astype(F32).astype(BF16)
        picked = dot_nn(hot, qg[...]).astype(BF16)
        q = jnp.concatenate([picked[:, h * DH : (h + 1) * DH] for h in range(REP)], axis=0)
        g = jnp.concatenate([picked[:, wide + h * DH : wide + (h + 1) * DH] for h in range(REP)], axis=0)
        valid = (base + lax.rem(iota((1, ROWS), 1), CHUNK) < count).astype(F32)

        def fold(x):
            parts = [x[8 * i : 8 * i + 8] for i in range(TILE // 8)]
            return parts

        def pass_a(t, top):
            off = pl.multiple_of(t * TILE, TILE)
            k = kvp[pl.ds(pl.multiple_of(off + BLOCK, BLOCK), TILE), :DH]
            s = dot_nt(k, q)
            sc[pl.ds(off, TILE), :] = s
            return jnp.maximum(top, jnp.max(s, axis=0, keepdims=True))

        top = lax.fori_loop(0, tiles, pass_a, jnp.full((1, ROWS), NEG, F32))

        def pass_b(t, state):
            total, dsum, mixed = state
            off = pl.multiple_of(t * TILE, TILE)
            v = kvp[pl.ds(pl.multiple_of(off + BLOCK, BLOCK), TILE), DH:]
            w = jnp.exp2((sc[pl.ds(off, TILE), :] - top) * EXP2)
            d = dot_nt(v, g)
            sc[pl.ds(off, TILE), :] = w
            dp[pl.ds(off, TILE), :] = d
            high = w.astype(BF16)
            low = (w - high.astype(F32)).astype(BF16)
            vt = kvt[DH:, pl.ds(off, TILE)]
            return (
                total + jnp.sum(w, axis=0, keepdims=True),
                dsum + jnp.sum(w * d, axis=0, keepdims=True),
                mixed + dot_nn(vt, high) + dot_nn(vt, low),
            )

        zero = jnp.zeros((1, ROWS), F32)
        total, dsum, mixed = lax.fori_loop(0, tiles, pass_b, (zero, zero, jnp.zeros((DH, ROWS), F32)))
        inv = 1.0 / total
        delta = dsum * inv
        inv_live = inv * valid

        def pass_c(t, gq):
            off = pl.multiple_of(t * TILE, TILE)
            here = pl.ds(pl.multiple_of(off + BLOCK, BLOCK), TILE)
            p = sc[pl.ds(off, TILE), :] * inv_live
            ds = (p * (dp[pl.ds(off, TILE), :] - delta)).astype(BF16)
            dkv[here, :DH] += dot_nn(ds, q) * SCALE
            dkv[here, DH:] += dot_nn(p.astype(BF16), g)
            return gq + dot_nn(kvt[:DH, pl.ds(off, TILE)], ds)

        gq = lax.fori_loop(0, tiles, pass_c, jnp.zeros((DH, ROWS), F32))
        att = (mixed * inv_live).T.astype(BF16)
        gqr = (gq * SCALE).T.astype(BF16)
        rows = pl.ds(pl.multiple_of(base, CHUNK), CHUNK)
        for h in range(REP):
            attg[rows, h * DH : (h + 1) * DH] = att[h * CHUNK : (h + 1) * CHUNK]
            attg[rows, wide + h * DH : wide + (h + 1) * DH] = gqr[h * CHUNK : (h + 1) * CHUNK]
        return carry

    lax.fori_loop(0, (count + CHUNK - 1) // CHUNK, chunk, 0)

    slots = attg.shape[0]

    def block(b, carry):
        base = pl.multiple_of(first + b * BLOCK, BLOCK)
        win = pl.ds(base, 3 * BLOCK)
        mine = pl.ds(pl.multiple_of(b * BLOCK, BLOCK), BLOCK)
        kn = kvp[win, :DH]
        vn = kvp[win, DH:]
        kf = kg[:, :DH]
        vf = kg[:, DH:]
        q = jnp.concatenate([qg[mine, h * DH : (h + 1) * DH] for h in range(REP)], axis=0)
        g = jnp.concatenate([qg[mine, wide + h * DH : wide + (h + 1) * DH] for h in range(REP)], axis=0)
        key_tok = base - BLOCK + iota((3 * BLOCK, 1), 0)
        key_glob = jnp.sum((key_tok == pos_row).astype(F32), axis=1, keepdims=True)
        usable = (key_tok >= 0) & (key_tok < seq) & (key_glob < 0.5)
        row_tok = base + lax.rem(iota((1, ROWS), 1), BLOCK)
        live = 1.0 - jnp.sum((pos_col == row_tok).astype(F32), axis=0, keepdims=True)

        sn = jnp.where(usable, dot_nt(kn, q), NEG)
        sf = dot_nt(kf, q)
        top = jnp.maximum(jnp.max(sn, axis=0, keepdims=True), jnp.max(sf, axis=0, keepdims=True))
        wn = jnp.exp2((sn - top) * EXP2)
        wf = jnp.exp2((sf - top) * EXP2)
        dn = dot_nt(vn, g)
        df = dot_nt(vf, g)
        total = jnp.sum(wn, axis=0, keepdims=True) + jnp.sum(wf, axis=0, keepdims=True)
        dsum = jnp.sum(wn * dn, axis=0, keepdims=True) + jnp.sum(wf * df, axis=0, keepdims=True)
        inv = 1.0 / total
        delta = dsum * inv
        knt = kn.T
        vnt = vn.T
        mixed = (dot_nn(vnt, wn.astype(BF16)) + dot_nn(kgt[DH:, :], wf.astype(BF16))) * inv
        inv_live = inv * live
        pn = wn * inv_live
        pf = wf * inv_live
        dsn = (pn * (dn - delta)).astype(BF16)
        dsf = (pf * (df - delta)).astype(BF16)
        gq = (dot_nn(knt, dsn) + dot_nn(kgt[:DH, :], dsf)) * SCALE
        dkv[win, :DH] += dot_nn(dsn, q) * SCALE
        dkv[win, DH:] += dot_nn(pn.astype(BF16), g)
        dkg[:, :DH] += dot_nn(dsf, q) * SCALE
        dkg[:, DH:] += dot_nn(pf.astype(BF16), g)

        tok_col = base + iota((BLOCK, 1), 0)
        is_col = jnp.sum((tok_col == pos_row).astype(F32), axis=1, keepdims=True) > 0.5
        rank = jnp.sum((pos_row < tok_col).astype(F32), axis=1, keepdims=True).astype(jnp.int32)
        hot = (jnp.where(is_col, rank - before, -1) == iota((BLOCK, slots), 1)).astype(F32).astype(BF16)
        placed = dot_nn(hot, attg[...])
        att = mixed.T
        gqr = gq.T
        for h in range(REP):
            lo, hi = h * DH, (h + 1) * DH
            rows = slice(h * BLOCK, (h + 1) * BLOCK)
            out[mine, lo:hi] = jnp.where(is_col, placed[:, lo:hi], att[rows]).astype(BF16)
            out[mine, wide + lo : wide + hi] = jnp.where(
                is_col, placed[:, wide + lo : wide + hi], gqr[rows]
            ).astype(BF16)
        return carry

    lax.fori_loop(0, ctoks // BLOCK, block, 0)

    out_copies = []
    for step in range(GROUP):
        dst = lax.rem(z + step, GROUP)
        copy = pltpu.make_async_copy(
            out.at[pl.ds(pl.multiple_of(dst * toks, toks), toks)], qg_out[step], out_sem.at[step]
        )
        copy.start()
        out_copies.append(copy)

    far = dkg[...]
    far_high = far.astype(BF16)
    far_low = (far - far_high.astype(F32)).astype(BF16)

    def finish(t, carry):
        off = pl.multiple_of(t * TILE, TILE)
        hot = (off + iota((TILE, glob), 0) == pos_row).astype(F32).astype(BF16)
        whole = dkv[pl.ds(pl.multiple_of(off + BLOCK, BLOCK), TILE), :] + dot_nn(hot, far_high) + dot_nn(hot, far_low)
        dkv_bf[pl.ds(off, TILE), :] = whole.astype(BF16)
        return carry

    lax.fori_loop(0, tiles, finish, 0)
    last = pltpu.make_async_copy(dkv_bf, dkv_out, dkv_sem)
    last.start()
    last.wait()
    for copy in out_copies:
        copy.wait()


def post_kernel(clusters, dkv_ref, o0, o1, o2, o3, att_ref, gq_ref, dk_ref, dv_ref):
    z = lax.rem(lax.axis_index("ctx"), GROUP)
    wide = REP * DH
    for step, o in enumerate((o0, o1, o2, o3)):
        col = pl.multiple_of(lax.rem(z + GROUP - step, GROUP) * wide, wide)
        att_ref[:, pl.ds(col, wide)] = o[:, :wide]
        gq_ref[:, pl.ds(col, wide)] = o[:, wide:]
    for j in range(HK):
        whole = dkv_ref[j].astype(F32)
        for s in range(1, clusters):
            whole = whole + dkv_ref[s * GROUP + j].astype(F32)
        dk_ref[:, j * DH : (j + 1) * DH] = whole[:, :DH].astype(BF16)
        dv_ref[:, j * DH : (j + 1) * DH] = whole[:, DH:].astype(BF16)


def local(queries, keys, values, grad_out, positions):
    toks, width = queries.shape
    kwidth = keys.shape[1]
    count = lax.axis_size("ctx")
    clusters = count // GROUP
    seq = toks * count
    glob = positions.shape[0]
    vmem = pl.BlockSpec(memory_space=pltpu.VMEM)
    smem = pl.BlockSpec(memory_space=pltpu.SMEM)
    anym = pl.BlockSpec(memory_space=pl.ANY)
    params = pltpu.CompilerParams(vmem_limit_bytes=60 * 1024 * 1024)
    part = jax.ShapeDtypeStruct((toks, 2 * REP * DH), BF16)

    kv_send, *qg_send = pl.pallas_call(
        functools.partial(prep_kernel, clusters),
        out_shape=(jax.ShapeDtypeStruct((count, toks, 2 * DH), BF16),) + (part,) * GROUP,
        in_specs=[vmem] * 4,
        out_specs=(vmem,) * (GROUP + 1),
        name="prep",
    )(queries, keys, values, grad_out)

    def shift(array, step):
        pairs = [(c, c // GROUP * GROUP + (c + step) % GROUP) for c in range(count)]
        return lax.ppermute(array, "ctx", pairs)

    qg_here = [qg_send[0]] + [shift(qg_send[step], step) for step in range(1, GROUP)]
    kv_all = lax.all_to_all(kv_send, "ctx", 0, 0, tiled=True).reshape(seq, 2 * DH)
    first = lax.axis_index("ctx") // GROUP * (GROUP * toks)
    edges = first + jnp.arange(2, dtype=jnp.int32) * (GROUP * toks)
    bounds = jnp.sum((positions[None, :] < edges[:, None]).astype(jnp.int32), axis=1)

    pad = seq + 2 * BLOCK
    ctoks = GROUP * toks
    slots = 2 * CHUNK
    dkv, *outs = pl.pallas_call(
        functools.partial(main_kernel, seq, toks, glob),
        out_shape=(jax.ShapeDtypeStruct((seq, 2 * DH), BF16),) + (part,) * GROUP,
        in_specs=[smem, vmem, anym] + [anym] * GROUP,
        out_specs=(anym,) * (GROUP + 1),
        scratch_shapes=[
            pltpu.VMEM((pad, 2 * DH), BF16),
            pltpu.VMEM((2 * DH, seq), BF16),
            pltpu.VMEM((pad, 2 * DH), F32),
            pltpu.VMEM((seq, 2 * DH), BF16),
            pltpu.VMEM((ctoks, 2 * REP * DH), BF16),
            pltpu.VMEM((ctoks, 2 * REP * DH), BF16),
            pltpu.VMEM((seq, ROWS), F32),
            pltpu.VMEM((seq, ROWS), F32),
            pltpu.VMEM((slots, 2 * REP * DH), BF16),
            pltpu.VMEM((glob, 2 * DH), BF16),
            pltpu.VMEM((2 * DH, glob), BF16),
            pltpu.VMEM((glob, 2 * DH), F32),
            pltpu.SemaphoreType.DMA,
            pltpu.SemaphoreType.DMA((GROUP,)),
            pltpu.SemaphoreType.DMA((GROUP,)),
            pltpu.SemaphoreType.DMA,
        ],
        compiler_params=params,
        name="attend",
    )(bounds, positions.reshape(1, glob), kv_all, *qg_here)

    out_here = [outs[0]] + [shift(outs[step], step) for step in range(1, GROUP)]
    back = lax.all_to_all(dkv.reshape(count, toks, 2 * DH), "ctx", 0, 0, tiled=True)
    return pl.pallas_call(
        functools.partial(post_kernel, clusters),
        out_shape=(
            jax.ShapeDtypeStruct((toks, width), BF16),
            jax.ShapeDtypeStruct((toks, width), BF16),
            jax.ShapeDtypeStruct((toks, kwidth), BF16),
            jax.ShapeDtypeStruct((toks, kwidth), BF16),
        ),
        in_specs=[vmem] * (GROUP + 1),
        out_specs=(vmem,) * 4,
        name="post",
    )(back, *out_here)


def solution(mesh):
    rows = P(("dp", "ctx"), None)
    return jax.shard_map(
        local,
        mesh=mesh,
        in_specs=(rows, rows, rows, rows, P("dp")),
        out_specs=(rows, rows, rows, rows),
        check_vma=False,
    )
```

```python
import functools
import math

import jax
import jax.numpy as jnp
from jax import lax
from jax.experimental import pallas as pl
from jax.experimental.pallas import tpu as pltpu
from jax.sharding import PartitionSpec as P

HQ = 16
HK = 4
DH = 128
BLOCK = 64
CAP = 32
REP = HQ // HK
GROUP = 4
SIDES = 2
XS = 4
CHUNK = 64
ROWS = REP * BLOCK
WIDE = REP * DH
KV = 2 * DH
PIECES = 2 * WIDE // KV
SCALE = 1.0 / math.sqrt(DH)
EXP2 = SCALE * math.log2(math.e)
NEG = -1e30

F32 = jnp.float32
BF16 = jnp.bfloat16


def dot_nt(a, b):
    return lax.dot_general(a, b, (((1,), (1,)), ((), ())), preferred_element_type=F32)


def dot_nn(a, b):
    return lax.dot_general(a, b, (((1,), (0,)), ((), ())), preferred_element_type=F32)


def iota(shape, dim):
    return lax.broadcasted_iota(jnp.int32, shape, dim)


def hot(mask):
    return mask.astype(F32).astype(BF16)


def split(x):
    high = x.astype(BF16)
    return high, (x - high.astype(F32)).astype(BF16)


def place():
    me = lax.axis_index("ctx")
    cluster = me // GROUP
    return me, cluster // SIDES, lax.rem(cluster, SIDES), lax.rem(me, GROUP)


def column(row):
    n = row.shape[1]
    eye = iota((n, n), 0) == iota((n, n), 1)
    wide = jnp.where(eye, jnp.broadcast_to(row, (n, n)), 0).astype(F32)
    return jnp.sum(wide, axis=1, keepdims=True).astype(jnp.int32)


def below(pos_row, edge):
    return jnp.sum((pos_row < edge).astype(F32), axis=1, keepdims=True).astype(jnp.int32)


def slots_along_lanes(pos_col, tok_row, before):
    is_row = jnp.sum((pos_col == tok_row).astype(F32), axis=0, keepdims=True)
    rank = jnp.sum((pos_col < tok_row).astype(F32), axis=0, keepdims=True).astype(jnp.int32)
    return jnp.where(is_row > 0.5, rank - before, -1)


def slots_along_rows(pos_row, tok_col, before):
    is_col = jnp.sum((pos_row == tok_col).astype(F32), axis=1, keepdims=True)
    rank = jnp.sum((pos_row < tok_col).astype(F32), axis=1, keepdims=True).astype(jnp.int32)
    return jnp.where(is_col > 0.5, rank - before, -1)


def prep_kernel(toks, pos_ref, q_ref, k_ref, v_ref, g_ref, *refs):
    zs_refs, qg_refs, picked = refs[:GROUP], refs[GROUP : 2 * GROUP], refs[2 * GROUP]
    me, x, y, z = place()
    pos_row = pos_ref[...]
    first = me * toks
    slot = slots_along_lanes(column(pos_row), first + iota((1, toks), 1), below(pos_row, first))
    pick = hot(slot == iota((CAP, toks), 0))
    width = HQ * DH
    picked[:, :width] = dot_nn(pick, q_ref[...]).astype(BF16)
    picked[:, width:] = dot_nn(pick, g_ref[...]).astype(BF16)
    for step in range(GROUP):
        j = lax.rem(z + step, GROUP)
        head = pl.ds(pl.multiple_of(j * DH, DH), DH)
        cols = pl.ds(pl.multiple_of(j * WIDE, WIDE), WIDE)
        zs_refs[step][:toks, :DH] = k_ref[:, head]
        zs_refs[step][:toks, DH:] = v_ref[:, head]
        for p in range(PIECES):
            base = j * WIDE + p * KV if p * KV < WIDE else width + j * WIDE + p * KV - WIDE
            part = picked[:, pl.ds(pl.multiple_of(base, KV), KV)]
            zs_refs[step][toks + CAP * p : toks + CAP * (p + 1), :] = part
        qg_refs[step][:, :WIDE] = q_ref[:, cols]
        qg_refs[step][:, WIDE:] = g_ref[:, cols]


def join_kernel(toks, *refs):
    zs_refs, kv_ref, qc_ref = refs[:GROUP], refs[GROUP], refs[GROUP + 1]
    me, x, y, z = place()
    for step in range(GROUP):
        src = lax.rem(z + GROUP - step, GROUP)
        kv_ref[pl.ds(pl.multiple_of(src * toks, toks), toks), :] = zs_refs[step][:toks, :]
        rows = PIECES * CAP
        qc_ref[pl.ds(pl.multiple_of(src * rows, rows), rows), :] = zs_refs[step][toks:, :]


def side_first(x, y, m, ctoks):
    return (lax.rem(x + XS - m, XS) * SIDES + y) * ctoks


def pick_kernel(ctoks, pos_ref, *refs):
    kv_refs, out_ref = refs[:XS], refs[XS]
    me, x, y, z = place()
    pos_row = pos_ref[...]
    glob = pos_row.shape[1]
    pos_col = column(pos_row)
    got = jnp.zeros((glob, KV), F32)
    for m in range(XS):
        first = side_first(x, y, m, ctoks)
        got = got + dot_nn(hot(pos_col == first + iota((glob, ctoks), 1)), kv_refs[m][...])
    out_ref[:glob, :] = got.astype(BF16)
    end = slice(ctoks - BLOCK, ctoks)
    out_ref[glob : glob + BLOCK, :] = jnp.where(y == 0, kv_refs[0][end, :], kv_refs[1][end, :])
    out_ref[glob + BLOCK : glob + 2 * BLOCK, :] = jnp.where(
        y == 0, kv_refs[3][:BLOCK, :], kv_refs[0][:BLOCK, :]
    )


def fill_slots(y, slots, mine_ref, peer_ref):
    half = GROUP * CAP
    rows = PIECES * CAP
    for ref, side in ((mine_ref, y), (peer_ref, 1 - y)):
        for d in range(GROUP):
            at = pl.ds(pl.multiple_of(side * half + d * CAP, CAP), CAP)
            for p in range(PIECES):
                begin = d * rows + p * CAP
                slots[at, p * KV : (p + 1) * KV] = ref[begin : begin + CAP, :]


def padded_ranks(x, toks, pos_row, pos_col, before):
    lane = iota((1, 2 * GROUP * CAP), 1)
    dev = x * (SIDES * GROUP) + lane // CAP
    start = jnp.sum((pos_col < dev * toks).astype(F32), axis=0, keepdims=True).astype(jnp.int32)
    stop = jnp.sum((pos_col < (dev + 1) * toks).astype(F32), axis=0, keepdims=True).astype(jnp.int32)
    rank = start + lax.rem(lane, CAP)
    return jnp.where(rank < stop, rank - before, -1)


def chunk_rows(slots, ranks, base):
    pick = hot(ranks == base + iota((CHUNK, ranks.shape[1]), 0))
    got = dot_nn(pick, slots[...]).astype(BF16)
    q = jnp.concatenate([got[:, h * DH : (h + 1) * DH] for h in range(REP)], axis=0)
    g = jnp.concatenate([got[:, WIDE + h * DH : WIDE + (h + 1) * DH] for h in range(REP)], axis=0)
    return q, g


def stats_kernel(toks, count_ref, pos_ref, *refs):
    kv_refs, mine_ref, peer_ref, out_ref = refs[:XS], refs[XS], refs[XS + 1], refs[XS + 2]
    slots, sc = refs[XS + 3 :]
    me, x, y, z = place()
    pos_row = pos_ref[...]
    before = below(pos_row, x * (SIDES * GROUP * toks))
    fill_slots(y, slots, mine_ref, peer_ref)
    ranks = padded_ranks(x, toks, pos_row, column(pos_row), before)
    ctoks = GROUP * toks
    out_ref[...] = jnp.zeros_like(out_ref)

    def chunk(ch, carry):
        q, g = chunk_rows(slots, ranks, ch * CHUNK)
        top = jnp.full((1, ROWS), NEG, F32)
        for m in range(XS):
            s = dot_nt(kv_refs[m][:, :DH], q)
            sc[m * ctoks : (m + 1) * ctoks, :] = s
            top = jnp.maximum(top, jnp.max(s, axis=0, keepdims=True))
        total = jnp.zeros((1, ROWS), F32)
        dsum = jnp.zeros((1, ROWS), F32)
        for m in range(XS):
            w = jnp.exp2((sc[m * ctoks : (m + 1) * ctoks, :] - top) * EXP2)
            total = total + jnp.sum(w, axis=0, keepdims=True)
            dsum = dsum + jnp.sum(w * dot_nt(kv_refs[m][:, DH:], g), axis=0, keepdims=True)
        out_ref[ch, 0:1, :] = top
        out_ref[ch, 1:2, :] = total
        out_ref[ch, 2:3, :] = dsum
        return carry

    lax.fori_loop(0, (count_ref[0] + CHUNK - 1) // CHUNK, chunk, 0)


def near_kernel(seq, toks, pos_ref, kv_ref, e2_ref, e2p_ref, *refs):
    qg_in = refs[:GROUP]
    outs = refs[GROUP : 2 * GROUP]
    dw_ref, dkg_ref, e5_ref, win, dwin, kg, kgt, qg, out = refs[2 * GROUP :]
    me, x, y, z = place()
    ctoks = GROUP * toks
    pos_row = pos_ref[...]
    glob = pos_row.shape[1]
    pos_col = column(pos_row)
    first = (me // GROUP) * ctoks
    win[:BLOCK, :] = e2p_ref[glob : glob + BLOCK, :]
    win[BLOCK : BLOCK + ctoks, :] = kv_ref[...]
    win[BLOCK + ctoks :, :] = e2p_ref[glob + BLOCK :, :]
    both = (e2_ref[:glob, :].astype(F32) + e2p_ref[:glob, :].astype(F32)).astype(BF16)
    kg[...] = both
    kgt[...] = both.T
    for step in range(GROUP):
        src = lax.rem(z + GROUP - step, GROUP)
        qg[pl.ds(pl.multiple_of(src * toks, toks), toks), :] = qg_in[step][...]
    dwin[...] = jnp.zeros_like(dwin)
    dkg_ref[...] = jnp.zeros_like(dkg_ref)

    def block(b, carry):
        base = first + b * BLOCK
        here = pl.ds(pl.multiple_of(b * BLOCK, BLOCK), 3 * BLOCK)
        mine = pl.ds(pl.multiple_of(b * BLOCK, BLOCK), BLOCK)
        kn, vn = win[here, :DH], win[here, DH:]
        q = jnp.concatenate([qg[mine, h * DH : (h + 1) * DH] for h in range(REP)], axis=0)
        g = jnp.concatenate([qg[mine, WIDE + h * DH : WIDE + (h + 1) * DH] for h in range(REP)], axis=0)
        key_tok = base - BLOCK + iota((3 * BLOCK, 1), 0)
        key_glob = jnp.sum((key_tok == pos_row).astype(F32), axis=1, keepdims=True)
        usable = (key_tok >= 0) & (key_tok < seq) & (key_glob < 0.5)
        row_tok = base + lax.rem(iota((1, ROWS), 1), BLOCK)
        live = 1.0 - jnp.sum((pos_col == row_tok).astype(F32), axis=0, keepdims=True)

        sn = jnp.where(usable, dot_nt(kn, q), NEG)
        sf = dot_nt(kg[:, :DH], q)
        top = jnp.maximum(jnp.max(sn, axis=0, keepdims=True), jnp.max(sf, axis=0, keepdims=True))
        wn = jnp.exp2((sn - top) * EXP2)
        wf = jnp.exp2((sf - top) * EXP2)
        dn = dot_nt(vn, g)
        df = dot_nt(kg[:, DH:], g)
        total = jnp.sum(wn, axis=0, keepdims=True) + jnp.sum(wf, axis=0, keepdims=True)
        dsum = jnp.sum(wn * dn, axis=0, keepdims=True) + jnp.sum(wf * df, axis=0, keepdims=True)
        inv = 1.0 / total
        delta = dsum * inv
        mixed = (dot_nn(vn.T, wn.astype(BF16)) + dot_nn(kgt[DH:, :], wf.astype(BF16))) * inv
        inv_live = inv * live
        pn = wn * inv_live
        pf = wf * inv_live
        dsn = (pn * (dn - delta)).astype(BF16)
        dsf = (pf * (df - delta)).astype(BF16)
        gq = (dot_nn(kn.T, dsn) + dot_nn(kgt[:DH, :], dsf)) * SCALE
        dwin[here, :DH] += dot_nn(dsn, q) * SCALE
        dwin[here, DH:] += dot_nn(pn.astype(BF16), g)
        dkg_ref[:, :DH] += dot_nn(dsf, q) * SCALE
        dkg_ref[:, DH:] += dot_nn(pf.astype(BF16), g)
        att = mixed.T.astype(BF16)
        gqr = gq.T.astype(BF16)
        for h in range(REP):
            rows = slice(h * BLOCK, (h + 1) * BLOCK)
            out[mine, h * DH : (h + 1) * DH] = att[rows]
            out[mine, WIDE + h * DH : WIDE + (h + 1) * DH] = gqr[rows]
        return carry

    lax.fori_loop(0, ctoks // BLOCK, block, 0)
    for step in range(GROUP):
        dst = lax.rem(z + step, GROUP)
        outs[step][...] = out[pl.ds(pl.multiple_of(dst * toks, toks), toks), :]
    dw_ref[...] = dwin[BLOCK : BLOCK + ctoks, :]
    e5_ref[:glob, :] = dkg_ref[...].astype(BF16)
    e5_ref[glob : glob + BLOCK, :] = dwin[:BLOCK, :].astype(BF16)
    e5_ref[glob + BLOCK :, :] = dwin[BLOCK + ctoks :, :].astype(BF16)


def grads_kernel(toks, count_ref, pos_ref, *refs):
    kv_refs, refs = refs[:XS], refs[XS:]
    mine_ref, peer_ref, st_ref, stp_ref, dw_ref, dkg_ref, e5p_ref = refs[:7]
    own_ref, send_refs, e4_ref, keep_ref = refs[7], refs[8 : 7 + XS], refs[7 + XS], refs[8 + XS]
    slots, dkv, kvt, rows_out = refs[9 + XS :]
    me, x, y, z = place()
    ctoks = GROUP * toks
    pos_row = pos_ref[...]
    glob = pos_row.shape[1]
    pos_col = column(pos_row)
    pair_first = x * (SIDES * ctoks)
    before = below(pos_row, pair_first)
    count = count_ref[0]
    fill_slots(y, slots, mine_ref, peer_ref)
    ranks = padded_ranks(x, toks, pos_row, pos_col, before)
    rows_out[...] = jnp.zeros_like(rows_out)
    for m in range(XS):
        kvt[m] = kv_refs[m][...].T

    far_high, far_low = split(dkg_ref[...] + e5p_ref[:glob, :].astype(F32))
    for m in range(XS):
        first = side_first(x, y, m, ctoks)
        mask = hot(first + iota((ctoks, glob), 0) == pos_row)
        whole = dot_nn(mask, far_high) + dot_nn(mask, far_low)
        dkv[m] = whole + dw_ref[...] if m == 0 else whole
    low = e5p_ref[glob : glob + BLOCK, :].astype(F32)
    high = e5p_ref[glob + BLOCK :, :].astype(F32)
    end = slice(ctoks - BLOCK, ctoks)
    at_zero = (y == 0).astype(F32)
    at_one = 1.0 - at_zero
    dkv[0, end, :] += low * at_zero
    dkv[1, end, :] += low * at_one
    dkv[3, :BLOCK, :] += high * at_zero
    dkv[0, :BLOCK, :] += high * at_one

    def chunk(ch, carry):
        base = ch * CHUNK
        q, g = chunk_rows(slots, ranks, base)
        valid = (base + lax.rem(iota((1, ROWS), 1), CHUNK) < count).astype(F32)
        here, there = st_ref[ch], stp_ref[ch]
        top = jnp.maximum(here[0:1], there[0:1])
        a = jnp.exp2((here[0:1] - top) * EXP2)
        b = jnp.exp2((there[0:1] - top) * EXP2)
        inv = 1.0 / (here[1:2] * a + there[1:2] * b)
        delta = (here[2:3] * a + there[2:3] * b) * inv
        inv = inv * valid
        att = jnp.zeros((DH, ROWS), F32)
        gq = jnp.zeros((DH, ROWS), F32)
        for m in range(XS):
            p = jnp.exp2((dot_nt(kv_refs[m][:, :DH], q) - top) * EXP2) * inv
            p_high, p_low = split(p)
            ds = (p * (dot_nt(kv_refs[m][:, DH:], g) - delta)).astype(BF16)
            dkv[m, :, :DH] += dot_nn(ds, q) * SCALE
            dkv[m, :, DH:] += dot_nn(p_high, g)
            vt = kvt[m, DH:, :]
            att = att + dot_nn(vt, p_high) + dot_nn(vt, p_low)
            gq = gq + dot_nn(kvt[m, :DH, :], ds)
        att = att.T
        gq = (gq * SCALE).T
        rows = pl.ds(pl.multiple_of(base, CHUNK), CHUNK)
        for h in range(REP):
            part = slice(h * CHUNK, (h + 1) * CHUNK)
            rows_out[rows, h * DH : (h + 1) * DH] = att[part]
            rows_out[rows, WIDE + h * DH : WIDE + (h + 1) * DH] = gq[part]
        return carry

    lax.fori_loop(0, (count + CHUNK - 1) // CHUNK, chunk, 0)
    own_ref[...] = dkv[0]
    for m in range(1, XS):
        send_refs[m - 1][...] = dkv[XS - m].astype(BF16)

    part_high, part_low = split(rows_out[...])
    slot = iota((GROUP * CAP, 2 * GROUP * CAP), 0)
    lane = iota((GROUP * CAP, 2 * GROUP * CAP), 1)

    def cluster_mask(side):
        begin = below(pos_row, pair_first + side * ctoks) - before
        size = below(pos_row, pair_first + (side + 1) * ctoks) - before - begin
        return hot((lane == begin + slot) & (slot < size))

    e4_ref[...] = dot_nn(cluster_mask(1 - y), part_high).astype(BF16)
    mask = cluster_mask(y)
    keep_ref[...] = dot_nn(mask, part_high) + dot_nn(mask, part_low)


def merge_kernel(toks, pos_ref, own_ref, *refs):
    got_refs, refs = refs[: XS - 1], refs[XS - 1 :]
    keep_ref, e4p_ref = refs[0], refs[1]
    zs_refs, whole = refs[2 : 2 + GROUP], refs[2 + GROUP]
    me, x, y, z = place()
    pos_row = pos_ref[...]
    total = own_ref[...]
    for ref in got_refs:
        total = total + ref[...].astype(F32)
    whole[...] = total.astype(BF16)
    rows = (keep_ref[...] + e4p_ref[...].astype(F32)).astype(BF16)
    first_dev = (me // GROUP) * GROUP
    before = below(pos_row, first_dev * toks)
    slot = iota((CAP, GROUP * CAP), 0)
    lane = iota((CAP, GROUP * CAP), 1)
    for step in range(GROUP):
        j = lax.rem(z + step, GROUP)
        zs_refs[step][:toks, :] = whole[pl.ds(pl.multiple_of(j * toks, toks), toks), :]
        begin = below(pos_row, (first_dev + j) * toks) - before
        size = below(pos_row, (first_dev + j + 1) * toks) - before - begin
        got = dot_nn(hot((lane == begin + slot) & (slot < size)), rows).astype(BF16)
        for p in range(PIECES):
            zs_refs[step][toks + CAP * p : toks + CAP * (p + 1), :] = got[:, p * KV : (p + 1) * KV]


def post_kernel(toks, pos_ref, *refs):
    zs_refs, o_refs = refs[:GROUP], refs[GROUP : 2 * GROUP]
    att_ref, gq_ref, dk_ref, dv_ref = refs[2 * GROUP :]
    me, x, y, z = place()
    pos_row = pos_ref[...]
    first = me * toks
    slot = slots_along_rows(pos_row, first + iota((toks, 1), 0), below(pos_row, first))
    mask = hot(slot == iota((toks, CAP), 1))
    is_glob = slot >= 0
    for step in range(GROUP):
        j = lax.rem(z + GROUP - step, GROUP)
        head = pl.ds(pl.multiple_of(j * DH, DH), DH)
        dk_ref[:, head] = zs_refs[step][:toks, :DH]
        dv_ref[:, head] = zs_refs[step][:toks, DH:]
        for p in range(PIECES):
            rows = zs_refs[step][toks + CAP * p : toks + CAP * (p + 1), :]
            placed = dot_nn(mask, rows)
            here = o_refs[step][:, p * KV : (p + 1) * KV].astype(F32)
            value = jnp.where(is_glob, placed, here).astype(BF16)
            ref, off = (att_ref, p * KV) if p * KV < WIDE else (gq_ref, p * KV - WIDE)
            ref[:, pl.ds(pl.multiple_of(j * WIDE + off, KV), KV)] = value


VM = pl.BlockSpec(memory_space=pltpu.VMEM)
SM = pl.BlockSpec(memory_space=pltpu.SMEM)


def call(kernel, name, outs, args, scratch=(), scalars=0, flops=0, moved=0):
    return pl.pallas_call(
        kernel,
        out_shape=tuple(jax.ShapeDtypeStruct(s, d) for s, d in outs),
        in_specs=[SM] * scalars + [VM] * (len(args) - scalars),
        out_specs=(VM,) * len(outs),
        scratch_shapes=[pltpu.VMEM(s, d) for s, d in scratch],
        compiler_params=pltpu.CompilerParams(vmem_limit_bytes=40 * 1024 * 1024),
        cost_estimate=pl.CostEstimate(flops=flops, bytes_accessed=moved, transcendentals=0),
        name=name,
    )(*args)


def local(queries, keys, values, grad_out, positions):
    toks, width = queries.shape
    kwidth = keys.shape[1]
    devices = lax.axis_size("ctx")
    seq = toks * devices
    ctoks = GROUP * toks
    glob = positions.shape[0]
    pos = positions.reshape(1, glob)
    zrows = toks + PIECES * CAP
    edge = lax.axis_index("ctx") // (SIDES * GROUP) * (SIDES * ctoks)
    in_pair = (positions >= edge) & (positions < edge + SIDES * ctoks)
    count = jnp.sum(in_pair.astype(jnp.int32)).reshape(1)
    part = ((toks, 2 * WIDE), BF16)
    zpart = ((zrows, KV), BF16)
    cpart = ((ctoks, KV), BF16)
    ppart = ((glob + 2 * BLOCK, KV), BF16)

    def zperm(a, step):
        pairs = [(c, c // GROUP * GROUP + (c + step) % GROUP) for c in range(devices)]
        return lax.ppermute(a, "ctx", pairs)

    def xperm(a, step):
        return lax.ppermute(a, "ctx", [(c, (c + step * SIDES * GROUP) % devices) for c in range(devices)])

    def yperm(a):
        return lax.ppermute(a, "ctx", [(c, c ^ GROUP) for c in range(devices)])

    sent = call(
        functools.partial(prep_kernel, toks),
        "prep",
        [zpart] * GROUP + [part] * GROUP,
        (pos, queries, keys, values, grad_out),
        scratch=[((CAP, 2 * width), BF16)],
        moved=4 << 20,
    )
    zs = [sent[0]] + [zperm(sent[step], step) for step in range(1, GROUP)]
    kv0, qc = call(
        functools.partial(join_kernel, toks), "join", [cpart, ((GROUP * PIECES * CAP, KV), BF16)], tuple(zs), moved=1 << 20
    )
    kvs = [kv0] + [xperm(kv0, m) for m in range(1, XS)]
    qcp = yperm(qc)
    qgs = [sent[GROUP]] + [zperm(sent[GROUP + step], step) for step in range(1, GROUP)]
    (e2,) = call(functools.partial(pick_kernel, ctoks), "pick", [ppart], (pos, *kvs), moved=6 << 20)
    e2p = yperm(e2)
    (st,) = call(
        functools.partial(stats_kernel, toks),
        "stats",
        [((glob // CHUNK, 8, ROWS), F32)],
        (count, pos, *kvs, qc, qcp),
        scratch=[((2 * GROUP * CAP, 2 * WIDE), BF16), ((XS * ctoks, ROWS), F32)],
        scalars=1,
        moved=14 << 20,
    )
    stp = yperm(st)
    *outs, dw, dkg, e5 = call(
        functools.partial(near_kernel, seq, toks),
        "near",
        [part] * GROUP + [((ctoks, KV), F32), ((glob, KV), F32), ppart],
        (pos, kv0, e2, e2p, *qgs),
        scratch=[
            ((ctoks + 2 * BLOCK, KV), BF16),
            ((ctoks + 2 * BLOCK, KV), F32),
            ((glob, KV), BF16),
            ((KV, glob), BF16),
            ((ctoks, 2 * WIDE), BF16),
            ((ctoks, 2 * WIDE), BF16),
        ],
        moved=40 << 20,
    )
    e5p = yperm(e5)
    os = [outs[0]] + [zperm(outs[step], step) for step in range(1, GROUP)]
    own, *rest = call(
        functools.partial(grads_kernel, toks),
        "grads",
        [((ctoks, KV), F32)] + [cpart] * (XS - 1) + [((GROUP * CAP, 2 * WIDE), BF16), ((GROUP * CAP, 2 * WIDE), F32)],
        (count, pos, *kvs, qc, qcp, st, stp, dw, dkg, e5p),
        scratch=[
            ((2 * GROUP * CAP, 2 * WIDE), BF16),
            ((XS, ctoks, KV), F32),
            ((XS, KV, ctoks), BF16),
            ((2 * GROUP * CAP, 2 * WIDE), F32),
        ],
        scalars=1,
        moved=24 << 20,
    )
    sends, e4, keep = rest[: XS - 1], rest[XS - 1], rest[XS]
    got = [xperm(sends[m - 1], m) for m in range(1, XS)]
    e4p = yperm(e4)
    zback = call(
        functools.partial(merge_kernel, toks),
        "merge",
        [zpart] * GROUP,
        (pos, own, *got, keep, e4p),
        scratch=[((ctoks, KV), BF16)],
        moved=3 << 20,
    )
    zr = [zback[0]] + [zperm(zback[step], step) for step in range(1, GROUP)]
    return call(
        functools.partial(post_kernel, toks),
        "post",
        [((toks, width), BF16)] * 2 + [((toks, kwidth), BF16)] * 2,
        (pos, *zr, *os),
        moved=4 << 20,
    )


def solution(mesh):
    rows = P(("dp", "ctx"), None)
    return jax.shard_map(
        local,
        mesh=mesh,
        in_specs=(rows, rows, rows, rows, P("dp")),
        out_specs=(rows, rows, rows, rows),
        check_vma=False,
    )
```

```python
import functools
import math

import jax
import jax.numpy as jnp
from jax import lax
from jax.experimental import pallas as pl
from jax.experimental.pallas import tpu as pltpu
from jax.sharding import PartitionSpec as P


HQ = 16
HK = 4
DH = 128
BLOCK = 64
CAP = 32
REP = HQ // HK
GROUP = 4
SIDES = 2
XS = 4
CHUNK = 64
ROWS = REP * BLOCK
WIDE = REP * DH
KV = 2 * DH
PIECES = 2 * WIDE // KV
SCALE = 1.0 / math.sqrt(DH)
EXP2 = SCALE * math.log2(math.e)
NEG = -1e30

F32 = jnp.float32
BF16 = jnp.bfloat16


def dot_nt(a, b):
    return lax.dot_general(a, b, (((1,), (1,)), ((), ())), preferred_element_type=F32)


def dot_nn(a, b):
    return lax.dot_general(a, b, (((1,), (0,)), ((), ())), preferred_element_type=F32)


def iota(shape, dim):
    return lax.broadcasted_iota(jnp.int32, shape, dim)


def hot(mask):
    return mask.astype(F32).astype(BF16)


def split(x):
    high = x.astype(BF16)
    return high, (x - high.astype(F32)).astype(BF16)


def place():
    me = lax.axis_index("ctx")
    cluster = me // GROUP
    return me, cluster // SIDES, lax.rem(cluster, SIDES), lax.rem(me, GROUP)


def column(row):
    n = row.shape[1]
    eye = iota((n, n), 0) == iota((n, n), 1)
    wide = jnp.where(eye, jnp.broadcast_to(row, (n, n)), 0).astype(F32)
    return jnp.sum(wide, axis=1, keepdims=True).astype(jnp.int32)


def below(pos_row, edge):
    return jnp.sum((pos_row < edge).astype(F32), axis=1, keepdims=True).astype(jnp.int32)


def pair_count(pos_row, x, toks):
    size = SIDES * GROUP * toks
    inside = (pos_row >= x * size) & (pos_row < (x + 1) * size)
    return jnp.sum(inside.astype(F32)).astype(jnp.int32)


def slots_along_lanes(pos_col, tok_row, before):
    is_row = jnp.sum((pos_col == tok_row).astype(F32), axis=0, keepdims=True)
    rank = jnp.sum((pos_col < tok_row).astype(F32), axis=0, keepdims=True).astype(jnp.int32)
    return jnp.where(is_row > 0.5, rank - before, -1)


def slots_along_rows(pos_row, tok_col, before):
    is_col = jnp.sum((pos_row == tok_col).astype(F32), axis=1, keepdims=True)
    rank = jnp.sum((pos_row < tok_col).astype(F32), axis=1, keepdims=True).astype(jnp.int32)
    return jnp.where(is_col > 0.5, rank - before, -1)


def prep_kernel(toks, pos_any, q_any, k_any, v_any, g_any, *refs):
    zs_refs, qg_refs, pos_out = refs[:GROUP], refs[GROUP : 2 * GROUP], refs[2 * GROUP]
    picked, pos_ref, q_ref, g_ref, k_ref, v_ref, sems = refs[2 * GROUP + 1 :]
    pos_copy = pltpu.make_async_copy(pos_any, pos_ref, sems.at[4])
    pos_copy.start()
    copies = [
        pltpu.make_async_copy(src, dst, sems.at[i])
        for i, (src, dst) in enumerate(((q_any, q_ref), (g_any, g_ref), (k_any, k_ref), (v_any, v_ref)))
    ]
    for copy in copies:
        copy.start()
    me, _, _, z = place()
    pos_copy.wait()
    pos_row = pos_ref[...]
    pos_out[...] = pos_row
    first = me * toks
    slot = slots_along_lanes(column(pos_row), first + iota((1, toks), 1), below(pos_row, first))
    pick = hot(slot == iota((CAP, toks), 0))
    width = HQ * DH
    for copy in copies:
        copy.wait()
    picked[:, :width] = dot_nn(pick, q_ref[...]).astype(BF16)
    picked[:, width:] = dot_nn(pick, g_ref[...]).astype(BF16)
    for step in range(GROUP):
        j = lax.rem(z + step, GROUP)
        head = pl.ds(pl.multiple_of(j * DH, DH), DH)
        cols = pl.ds(pl.multiple_of(j * WIDE, WIDE), WIDE)
        zs_refs[step][:toks, :DH] = k_ref[:, head]
        zs_refs[step][:toks, DH:] = v_ref[:, head]
        for p in range(PIECES):
            base = j * WIDE + p * KV if p * KV < WIDE else width + j * WIDE + p * KV - WIDE
            part = picked[:, pl.ds(pl.multiple_of(base, KV), KV)]
            zs_refs[step][toks + CAP * p : toks + CAP * (p + 1), :] = part
        qg_refs[step][:, :WIDE] = q_ref[:, cols]
        qg_refs[step][:, WIDE:] = g_ref[:, cols]


def join_kernel(toks, *refs):
    zs_refs, kv_ref, qc_ref = refs[:GROUP], refs[GROUP], refs[GROUP + 1]
    _, _, _, z = place()
    for step in range(GROUP):
        src = lax.rem(z + GROUP - step, GROUP)
        kv_ref[pl.ds(pl.multiple_of(src * toks, toks), toks), :] = zs_refs[step][:toks, :]
        rows = PIECES * CAP
        qc_ref[pl.ds(pl.multiple_of(src * rows, rows), rows), :] = zs_refs[step][toks:, :]


def side_first(x, y, m, ctoks):
    return (lax.rem(x + XS - m, XS) * SIDES + y) * ctoks


def pick_kernel(ctoks, pos_ref, *refs):
    kv_refs, out_ref = refs[:XS], refs[XS]
    _, x, y, _ = place()
    pos_row = pos_ref[...]
    glob = pos_row.shape[1]
    pos_col = column(pos_row)
    got = jnp.zeros((glob, KV), F32)
    for m in range(XS):
        first = side_first(x, y, m, ctoks)
        got = got + dot_nn(hot(pos_col == first + iota((glob, ctoks), 1)), kv_refs[m][...])
    out_ref[:glob, :] = got.astype(BF16)
    end = slice(ctoks - BLOCK, ctoks)
    out_ref[glob : glob + BLOCK, :] = jnp.where(y == 0, kv_refs[0][end, :], kv_refs[1][end, :])
    out_ref[glob + BLOCK : glob + 2 * BLOCK, :] = jnp.where(
        y == 0, kv_refs[3][:BLOCK, :], kv_refs[0][:BLOCK, :]
    )


def fill_slots(y, slots, mine_ref, peer_ref):
    half = GROUP * CAP
    rows = PIECES * CAP
    for ref, side in ((mine_ref, y), (peer_ref, 1 - y)):
        for d in range(GROUP):
            at = pl.ds(pl.multiple_of(side * half + d * CAP, CAP), CAP)
            for p in range(PIECES):
                begin = d * rows + p * CAP
                slots[at, p * KV : (p + 1) * KV] = ref[begin : begin + CAP, :]


def padded_ranks(x, toks, pos_col, before):
    lane = iota((1, 2 * GROUP * CAP), 1)
    dev = x * (SIDES * GROUP) + lane // CAP
    start = jnp.sum((pos_col < dev * toks).astype(F32), axis=0, keepdims=True).astype(jnp.int32)
    stop = jnp.sum((pos_col < (dev + 1) * toks).astype(F32), axis=0, keepdims=True).astype(jnp.int32)
    rank = start + lax.rem(lane, CAP)
    return jnp.where(rank < stop, rank - before, -1)


def chunk_rows(slots, ranks, base):
    pick = hot(ranks == base + iota((CHUNK, ranks.shape[1]), 0))
    got = dot_nn(pick, slots[...]).astype(BF16)
    q = jnp.concatenate([got[:, h * DH : (h + 1) * DH] for h in range(REP)], axis=0)
    g = jnp.concatenate([got[:, WIDE + h * DH : WIDE + (h + 1) * DH] for h in range(REP)], axis=0)
    return q, g


def stats_kernel(toks, pos_ref, *refs):
    kv_refs, mine_ref, peer_ref, out_ref = refs[:XS], refs[XS], refs[XS + 1], refs[XS + 2]
    slots, sc = refs[XS + 3 :]
    _, x, y, _ = place()
    pos_row = pos_ref[...]
    before = below(pos_row, x * (SIDES * GROUP * toks))
    fill_slots(y, slots, mine_ref, peer_ref)
    ranks = padded_ranks(x, toks, column(pos_row), before)
    ctoks = GROUP * toks
    out_ref[...] = jnp.zeros_like(out_ref)

    def chunk(ch, carry):
        q, g = chunk_rows(slots, ranks, ch * CHUNK)
        top = jnp.full((1, ROWS), NEG, F32)
        for m in range(XS):
            s = dot_nt(kv_refs[m][:, :DH], q)
            sc[m * ctoks : (m + 1) * ctoks, :] = s
            top = jnp.maximum(top, jnp.max(s, axis=0, keepdims=True))
        total = jnp.zeros((1, ROWS), F32)
        dsum = jnp.zeros((1, ROWS), F32)
        for m in range(XS):
            w = jnp.exp2((sc[m * ctoks : (m + 1) * ctoks, :] - top) * EXP2)
            total = total + jnp.sum(w, axis=0, keepdims=True)
            dsum = dsum + jnp.sum(w * dot_nt(kv_refs[m][:, DH:], g), axis=0, keepdims=True)
        out_ref[ch, 0:1, :] = top
        out_ref[ch, 1:2, :] = total
        out_ref[ch, 2:3, :] = dsum
        return carry

    lax.fori_loop(0, (pair_count(pos_row, x, toks) + CHUNK - 1) // CHUNK, chunk, 0)


def near_kernel(seq, toks, pos_ref, after_ref, kv_ref, e2_ref, e2p_ref, *refs):
    qg_in = refs[:GROUP]
    outs = refs[GROUP : 2 * GROUP]
    dw_ref, dkg_ref, e5_ref, win, dwin, kg, kgt, qg, out = refs[2 * GROUP :]
    me, _, _, z = place()
    ctoks = GROUP * toks
    pos_row = pos_ref[...]
    glob = pos_row.shape[1]
    pos_col = column(pos_row)
    first = (me // GROUP) * ctoks
    win[:BLOCK, :] = e2p_ref[glob : glob + BLOCK, :]
    win[BLOCK : BLOCK + ctoks, :] = kv_ref[...]
    win[BLOCK + ctoks :, :] = e2p_ref[glob + BLOCK :, :]
    both = (e2_ref[:glob, :].astype(F32) + e2p_ref[:glob, :].astype(F32)).astype(BF16)
    kg[...] = both
    kgt[...] = both.T
    for step in range(GROUP):
        src = lax.rem(z + GROUP - step, GROUP)
        qg[pl.ds(pl.multiple_of(src * toks, toks), toks), :] = qg_in[step][...]
    dwin[...] = jnp.zeros_like(dwin)
    dkg_ref[...] = jnp.zeros_like(dkg_ref)

    def block(b, carry):
        base = first + b * BLOCK
        here = pl.ds(pl.multiple_of(b * BLOCK, BLOCK), 3 * BLOCK)
        mine = pl.ds(pl.multiple_of(b * BLOCK, BLOCK), BLOCK)
        kn, vn = win[here, :DH], win[here, DH:]
        q = jnp.concatenate([qg[mine, h * DH : (h + 1) * DH] for h in range(REP)], axis=0)
        g = jnp.concatenate([qg[mine, WIDE + h * DH : WIDE + (h + 1) * DH] for h in range(REP)], axis=0)
        key_tok = base - BLOCK + iota((3 * BLOCK, 1), 0)
        key_glob = jnp.sum((key_tok == pos_row).astype(F32), axis=1, keepdims=True)
        usable = (key_tok >= 0) & (key_tok < seq) & (key_glob < 0.5)
        row_tok = base + lax.rem(iota((1, ROWS), 1), BLOCK)
        live = 1.0 - jnp.sum((pos_col == row_tok).astype(F32), axis=0, keepdims=True)

        sn = jnp.where(usable, dot_nt(kn, q), NEG)
        sf = dot_nt(kg[:, :DH], q)
        top = jnp.maximum(jnp.max(sn, axis=0, keepdims=True), jnp.max(sf, axis=0, keepdims=True))
        wn = jnp.exp2((sn - top) * EXP2)
        wf = jnp.exp2((sf - top) * EXP2)
        dn = dot_nt(vn, g)
        df = dot_nt(kg[:, DH:], g)
        total = jnp.sum(wn, axis=0, keepdims=True) + jnp.sum(wf, axis=0, keepdims=True)
        dsum = jnp.sum(wn * dn, axis=0, keepdims=True) + jnp.sum(wf * df, axis=0, keepdims=True)
        inv = 1.0 / total
        delta = dsum * inv
        mixed = (dot_nn(vn.T, wn.astype(BF16)) + dot_nn(kgt[DH:, :], wf.astype(BF16))) * inv
        inv_live = inv * live
        pn = wn * inv_live
        pf = wf * inv_live
        dsn = (pn * (dn - delta)).astype(BF16)
        dsf = (pf * (df - delta)).astype(BF16)
        gq = (dot_nn(kn.T, dsn) + dot_nn(kgt[:DH, :], dsf)) * SCALE
        dwin[here, :DH] += dot_nn(dsn, q) * SCALE
        dwin[here, DH:] += dot_nn(pn.astype(BF16), g)
        dkg_ref[:, :DH] += dot_nn(dsf, q) * SCALE
        dkg_ref[:, DH:] += dot_nn(pf.astype(BF16), g)
        att = mixed.T.astype(BF16)
        gqr = gq.T.astype(BF16)
        for h in range(REP):
            rows = slice(h * BLOCK, (h + 1) * BLOCK)
            out[mine, h * DH : (h + 1) * DH] = att[rows]
            out[mine, WIDE + h * DH : WIDE + (h + 1) * DH] = gqr[rows]
        return carry

    lax.fori_loop(0, ctoks // BLOCK, block, 0)
    for step in range(GROUP):
        dst = lax.rem(z + step, GROUP)
        outs[step][...] = out[pl.ds(pl.multiple_of(dst * toks, toks), toks), :]
    dw_ref[...] = dwin[BLOCK : BLOCK + ctoks, :]
    e5_ref[:glob, :] = dkg_ref[...].astype(BF16)
    e5_ref[glob : glob + BLOCK, :] = dwin[:BLOCK, :].astype(BF16)
    e5_ref[glob + BLOCK :, :] = dwin[BLOCK + ctoks :, :].astype(BF16)


def grads_kernel(toks, pos_ref, *refs):
    kv_refs, refs = refs[:XS], refs[XS:]
    mine_ref, peer_ref, st_ref, stp_ref, dw_ref, dkg_ref = refs[:6]
    dkv, e4_ref, keep_ref, slots, kvt, rows_out = refs[6:]
    _, x, y, _ = place()
    ctoks = GROUP * toks
    pos_row = pos_ref[...]
    glob = pos_row.shape[1]
    pos_col = column(pos_row)
    pair_first = x * (SIDES * ctoks)
    before = below(pos_row, pair_first)
    count = pair_count(pos_row, x, toks)
    fill_slots(y, slots, mine_ref, peer_ref)
    ranks = padded_ranks(x, toks, pos_col, before)
    rows_out[...] = jnp.zeros_like(rows_out)
    for m in range(XS):
        kvt[m] = kv_refs[m][...].T

    far_high, far_low = split(dkg_ref[...])
    for m in range(XS):
        first = side_first(x, y, m, ctoks)
        mask = hot(first + iota((ctoks, glob), 0) == pos_row)
        whole = dot_nn(mask, far_high) + dot_nn(mask, far_low)
        dkv[m] = whole + dw_ref[...] if m == 0 else whole

    def chunk(ch, carry):
        base = ch * CHUNK
        q, g = chunk_rows(slots, ranks, base)
        valid = (base + lax.rem(iota((1, ROWS), 1), CHUNK) < count).astype(F32)
        here, there = st_ref[ch], stp_ref[ch]
        top = jnp.maximum(here[0:1], there[0:1])
        a = jnp.exp2((here[0:1] - top) * EXP2)
        b = jnp.exp2((there[0:1] - top) * EXP2)
        inv = 1.0 / (here[1:2] * a + there[1:2] * b)
        delta = (here[2:3] * a + there[2:3] * b) * inv
        inv = inv * valid
        att = jnp.zeros((DH, ROWS), F32)
        gq = jnp.zeros((DH, ROWS), F32)
        for m in range(XS):
            p = jnp.exp2((dot_nt(kv_refs[m][:, :DH], q) - top) * EXP2) * inv
            p_high, p_low = split(p)
            ds = (p * (dot_nt(kv_refs[m][:, DH:], g) - delta)).astype(BF16)
            dkv[m, :, :DH] += dot_nn(ds, q) * SCALE
            dkv[m, :, DH:] += dot_nn(p_high, g)
            vt = kvt[m, DH:, :]
            att = att + dot_nn(vt, p_high) + dot_nn(vt, p_low)
            gq = gq + dot_nn(kvt[m, :DH, :], ds)
        att = att.T
        gq = (gq * SCALE).T
        rows = pl.ds(pl.multiple_of(base, CHUNK), CHUNK)
        for h in range(REP):
            part = slice(h * CHUNK, (h + 1) * CHUNK)
            rows_out[rows, h * DH : (h + 1) * DH] = att[part]
            rows_out[rows, WIDE + h * DH : WIDE + (h + 1) * DH] = gq[part]
        return carry

    lax.fori_loop(0, (count + CHUNK - 1) // CHUNK, chunk, 0)
    part_high, part_low = split(rows_out[...])
    slot = iota((GROUP * CAP, 2 * GROUP * CAP), 0)
    lane = iota((GROUP * CAP, 2 * GROUP * CAP), 1)

    def cluster_mask(side):
        begin = below(pos_row, pair_first + side * ctoks) - before
        size = below(pos_row, pair_first + (side + 1) * ctoks) - before - begin
        return hot((lane == begin + slot) & (slot < size))

    e4_ref[...] = dot_nn(cluster_mask(1 - y), part_high).astype(BF16)
    mask = cluster_mask(y)
    keep_ref[...] = dot_nn(mask, part_high) + dot_nn(mask, part_low)


def peer_kernel(toks, pos_ref, dkv_ref, e5p_ref, own_ref, *send_refs):
    _, x, y, _ = place()
    ctoks = GROUP * toks
    pos_row = pos_ref[...]
    glob = pos_row.shape[1]
    far = e5p_ref[:glob, :]
    low = e5p_ref[glob : glob + BLOCK, :].astype(F32)
    high = e5p_ref[glob + BLOCK :, :].astype(F32)
    at_zero = (y == 0).astype(F32)
    at_one = 1.0 - at_zero
    none = jnp.zeros((ctoks - BLOCK, KV), F32)
    edges = {
        0: jnp.concatenate([high * at_one, none[BLOCK:], low * at_zero], axis=0),
        1: jnp.concatenate([none, low * at_one], axis=0),
        3: jnp.concatenate([high * at_zero, none], axis=0),
    }
    for m in range(XS):
        first = side_first(x, y, m, ctoks)
        mask = hot(first + iota((ctoks, glob), 0) == pos_row)
        whole = dkv_ref[m] + dot_nn(mask, far)
        if m in edges:
            whole = whole + edges[m]
        if m == 0:
            own_ref[...] = whole
        else:
            send_refs[XS - m - 1][...] = whole.astype(BF16)


def merge_kernel(toks, pos_ref, own_ref, *refs):
    got_refs, refs = refs[: XS - 1], refs[XS - 1 :]
    keep_ref, e4p_ref = refs[0], refs[1]
    zs_refs, whole = refs[2 : 2 + GROUP], refs[2 + GROUP]
    me, _, _, z = place()
    pos_row = pos_ref[...]
    total = own_ref[...]
    for ref in got_refs:
        total = total + ref[...].astype(F32)
    whole[...] = total.astype(BF16)
    rows = (keep_ref[...] + e4p_ref[...].astype(F32)).astype(BF16)
    first_dev = (me // GROUP) * GROUP
    before = below(pos_row, first_dev * toks)
    slot = iota((CAP, GROUP * CAP), 0)
    lane = iota((CAP, GROUP * CAP), 1)
    for step in range(GROUP):
        j = lax.rem(z + step, GROUP)
        zs_refs[step][:toks, :] = whole[pl.ds(pl.multiple_of(j * toks, toks), toks), :]
        begin = below(pos_row, (first_dev + j) * toks) - before
        size = below(pos_row, (first_dev + j + 1) * toks) - before - begin
        got = dot_nn(hot((lane == begin + slot) & (slot < size)), rows).astype(BF16)
        for p in range(PIECES):
            zs_refs[step][toks + CAP * p : toks + CAP * (p + 1), :] = got[:, p * KV : (p + 1) * KV]


def post_kernel(toks, pos_ref, *refs):
    zs_refs, o_refs = refs[:GROUP], refs[GROUP : 2 * GROUP]
    att_ref, gq_ref, dk_ref, dv_ref = refs[2 * GROUP :]
    me, _, _, z = place()
    pos_row = pos_ref[...]
    first = me * toks
    slot = slots_along_rows(pos_row, first + iota((toks, 1), 0), below(pos_row, first))
    mask = hot(slot == iota((toks, CAP), 1))
    is_glob = slot >= 0
    for step in range(GROUP):
        j = lax.rem(z + GROUP - step, GROUP)
        head = pl.ds(pl.multiple_of(j * DH, DH), DH)
        dk_ref[:, head] = zs_refs[step][:toks, :DH]
        dv_ref[:, head] = zs_refs[step][:toks, DH:]
        for p in range(PIECES):
            rows = zs_refs[step][toks + CAP * p : toks + CAP * (p + 1), :]
            placed = dot_nn(mask, rows)
            here = o_refs[step][:, p * KV : (p + 1) * KV].astype(F32)
            value = jnp.where(is_glob, placed, here).astype(BF16)
            ref, off = (att_ref, p * KV) if p * KV < WIDE else (gq_ref, p * KV - WIDE)
            ref[:, pl.ds(pl.multiple_of(j * WIDE + off, KV), KV)] = value


VM = pl.BlockSpec(memory_space=pltpu.VMEM)
HBM = pl.BlockSpec(memory_space=pltpu.HBM)


def call(kernel, outs, args, scratch=(), specs=None, sems=0, flops=0, moved=0):
    return pl.pallas_call(
        kernel,
        out_shape=tuple(jax.ShapeDtypeStruct(s, d) for s, d in outs),
        in_specs=specs or [VM] * len(args),
        out_specs=(VM,) * len(outs),
        scratch_shapes=[pltpu.VMEM(s, d) for s, d in scratch] + [pltpu.SemaphoreType.DMA((sems,))] * (sems > 0),
        compiler_params=pltpu.CompilerParams(vmem_limit_bytes=40 * 1024 * 1024),
        cost_estimate=pl.CostEstimate(flops=flops, bytes_accessed=moved, transcendentals=0),
    )(*args)


def local(queries, keys, values, grad_out, positions):
    toks, width = queries.shape
    kwidth = keys.shape[1]
    devices = lax.axis_size("ctx")
    seq = toks * devices
    ctoks = GROUP * toks
    glob = positions.shape[0]
    zrows = toks + PIECES * CAP
    part = ((toks, 2 * WIDE), BF16)
    zpart = ((zrows, KV), BF16)
    cpart = ((ctoks, KV), BF16)
    ppart = ((glob + 2 * BLOCK, KV), BF16)

    def zperm(a, step):
        pairs = [(c, c // GROUP * GROUP + (c + step) % GROUP) for c in range(devices)]
        return lax.ppermute(a, "ctx", pairs)

    def xperm(a, step):
        return lax.ppermute(a, "ctx", [(c, (c + step * SIDES * GROUP) % devices) for c in range(devices)])

    def yperm(a):
        return lax.ppermute(a, "ctx", [(c, c ^ GROUP) for c in range(devices)])

    sent = call(
        functools.partial(prep_kernel, toks),
        [zpart] * GROUP + [part] * GROUP + [((1, glob), jnp.int32)],
        tuple(pltpu.with_memory_space_constraint(a, pltpu.HBM) for a in (positions.reshape(1, glob), queries, keys, values, grad_out)),
        scratch=[
            ((CAP, 2 * width), BF16),
            ((1, glob), jnp.int32),
            ((toks, width), BF16),
            ((toks, width), BF16),
            ((toks, kwidth), BF16),
            ((toks, kwidth), BF16),
        ],
        specs=[HBM] * 5,
        sems=5,
        moved=4 << 20,
    )
    pos = sent[2 * GROUP]
    zs = [sent[0]] + [zperm(sent[step], step) for step in range(1, GROUP)]
    kv0, qc = call(
        functools.partial(join_kernel, toks), [cpart, ((GROUP * PIECES * CAP, KV), BF16)], tuple(zs), moved=1 << 20
    )
    kvs = [kv0] + [xperm(kv0, m) for m in range(1, XS)]
    qcp = yperm(qc)
    qgs = [sent[GROUP]] + [zperm(sent[GROUP + step], step) for step in range(1, GROUP)]
    (e2,) = call(functools.partial(pick_kernel, ctoks), [ppart], (pos, *kvs), moved=6 << 20)
    e2p = yperm(e2)
    (st,) = call(
        functools.partial(stats_kernel, toks),
        [((glob // CHUNK, 8, ROWS), F32)],
        (pos, *kvs, qc, qcp),
        scratch=[((2 * GROUP * CAP, 2 * WIDE), BF16), ((XS * ctoks, ROWS), F32)],
        moved=14 << 20,
    )
    stp = yperm(st)
    *outs, dw, dkg, e5 = call(
        functools.partial(near_kernel, seq, toks),
        [part] * GROUP + [((ctoks, KV), F32), ((glob, KV), F32), ppart],
        (pos, st, kv0, e2, e2p, *qgs),
        scratch=[
            ((ctoks + 2 * BLOCK, KV), BF16),
            ((ctoks + 2 * BLOCK, KV), F32),
            ((glob, KV), BF16),
            ((KV, glob), BF16),
            ((ctoks, 2 * WIDE), BF16),
            ((ctoks, 2 * WIDE), BF16),
        ],
        moved=40 << 20,
    )
    e5p = yperm(e5)
    os = [outs[0]] + [zperm(outs[step], step) for step in range(1, GROUP)]
    dkv, e4, keep = call(
        functools.partial(grads_kernel, toks),
        [((XS, ctoks, KV), F32), ((GROUP * CAP, 2 * WIDE), BF16), ((GROUP * CAP, 2 * WIDE), F32)],
        (pos, *kvs, qc, qcp, st, stp, dw, dkg),
        scratch=[
            ((2 * GROUP * CAP, 2 * WIDE), BF16),
            ((XS, KV, ctoks), BF16),
            ((2 * GROUP * CAP, 2 * WIDE), F32),
        ],
        moved=24 << 20,
    )
    own, *sends = call(
        functools.partial(peer_kernel, toks),
        [((ctoks, KV), F32)] + [cpart] * (XS - 1),
        (pos, dkv, e5p),
        moved=3 << 20,
    )
    got = [xperm(sends[m - 1], m) for m in range(1, XS)]
    e4p = yperm(e4)
    zback = call(
        functools.partial(merge_kernel, toks),
        [zpart] * GROUP,
        (pos, own, *got, keep, e4p),
        scratch=[((ctoks, KV), BF16)],
        moved=3 << 20,
    )
    zr = [zback[0]] + [zperm(zback[step], step) for step in range(1, GROUP)]
    return call(
        functools.partial(post_kernel, toks),
        [((toks, width), BF16)] * 2 + [((toks, kwidth), BF16)] * 2,
        (pos, *zr, *os),
        moved=4 << 20,
    )


def solution(mesh):
    rows = P(("dp", "ctx"), None)
    return jax.shard_map(
        local,
        mesh=mesh,
        in_specs=(rows, rows, rows, rows, P("dp")),
        out_specs=(rows, rows, rows, rows),
        check_vma=False,
    )
```

```python
import functools
import math

import jax
import jax.numpy as jnp
from jax import lax
from jax.experimental import pallas as pl
from jax.experimental.pallas import tpu as pltpu
from jax.sharding import PartitionSpec as P


HQ = 16
HK = 4
DH = 128
BLOCK = 64
CAP = 32
REP = HQ // HK
GROUP = 4
SIDES = 2
XS = 4
CHUNK = 128
ROWS = REP * BLOCK
GROWS = REP * CHUNK
WIDE = REP * DH
KV = 2 * DH
PIECES = 2 * WIDE // KV
SCALE = 1.0 / math.sqrt(DH)
EXP2 = SCALE * math.log2(math.e)
NEG = -1e30

F32 = jnp.float32
BF16 = jnp.bfloat16


def dot_nt(a, b):
    return lax.dot_general(a, b, (((1,), (1,)), ((), ())), preferred_element_type=F32)


def dot_nn(a, b):
    return lax.dot_general(a, b, (((1,), (0,)), ((), ())), preferred_element_type=F32)


def iota(shape, dim):
    return lax.broadcasted_iota(jnp.int32, shape, dim)


def hot(mask):
    return mask.astype(F32).astype(BF16)


def split(x):
    high = x.astype(BF16)
    return high, (x - high.astype(F32)).astype(BF16)


def place():
    me = lax.axis_index("ctx")
    cluster = me // GROUP
    return me, cluster // SIDES, lax.rem(cluster, SIDES), lax.rem(me, GROUP)


def column(row):
    n = row.shape[1]
    eye = iota((n, n), 0) == iota((n, n), 1)
    wide = jnp.where(eye, jnp.broadcast_to(row, (n, n)), 0).astype(F32)
    return jnp.sum(wide, axis=1, keepdims=True).astype(jnp.int32)


def below(pos_row, edge):
    return jnp.sum((pos_row < edge).astype(F32), axis=1, keepdims=True).astype(jnp.int32)


def pair_count(pos_row, x, toks):
    size = SIDES * GROUP * toks
    inside = (pos_row >= x * size) & (pos_row < (x + 1) * size)
    return jnp.sum(inside.astype(F32)).astype(jnp.int32)


def slots_along_lanes(pos_col, tok_row, before):
    is_row = jnp.sum((pos_col == tok_row).astype(F32), axis=0, keepdims=True)
    rank = jnp.sum((pos_col < tok_row).astype(F32), axis=0, keepdims=True).astype(jnp.int32)
    return jnp.where(is_row > 0.5, rank - before, -1)


def slots_along_rows(pos_row, tok_col, before):
    is_col = jnp.sum((pos_row == tok_col).astype(F32), axis=1, keepdims=True)
    rank = jnp.sum((pos_row < tok_col).astype(F32), axis=1, keepdims=True).astype(jnp.int32)
    return jnp.where(is_col > 0.5, rank - before, -1)


def prep_kernel(toks, pos_any, q_any, k_any, v_any, g_any, *refs):
    zs_refs, qg_refs, pos_out = refs[:GROUP], refs[GROUP : 2 * GROUP], refs[2 * GROUP]
    picked, pos_ref, q_ref, g_ref, k_ref, v_ref, sems = refs[2 * GROUP + 1 :]
    pos_copy = pltpu.make_async_copy(pos_any, pos_ref, sems.at[4])
    pos_copy.start()
    copies = [
        pltpu.make_async_copy(src, dst, sems.at[i])
        for i, (src, dst) in enumerate(((q_any, q_ref), (g_any, g_ref), (k_any, k_ref), (v_any, v_ref)))
    ]
    for copy in copies:
        copy.start()
    me, _, _, z = place()
    pos_copy.wait()
    pos_row = pos_ref[...]
    pos_out[...] = pos_row
    first = me * toks
    slot = slots_along_lanes(column(pos_row), first + iota((1, toks), 1), below(pos_row, first))
    pick = hot(slot == iota((CAP, toks), 0))
    width = HQ * DH
    for copy in copies:
        copy.wait()
    picked[:, :width] = dot_nn(pick, q_ref[...]).astype(BF16)
    picked[:, width:] = dot_nn(pick, g_ref[...]).astype(BF16)
    for step in range(GROUP):
        j = lax.rem(z + step, GROUP)
        head = pl.ds(pl.multiple_of(j * DH, DH), DH)
        cols = pl.ds(pl.multiple_of(j * WIDE, WIDE), WIDE)
        zs_refs[step][:toks, :DH] = k_ref[:, head]
        zs_refs[step][:toks, DH:] = v_ref[:, head]
        for p in range(PIECES):
            base = j * WIDE + p * KV if p * KV < WIDE else width + j * WIDE + p * KV - WIDE
            part = picked[:, pl.ds(pl.multiple_of(base, KV), KV)]
            zs_refs[step][toks + CAP * p : toks + CAP * (p + 1), :] = part
        qg_refs[step][:, :WIDE] = q_ref[:, cols]
        qg_refs[step][:, WIDE:] = g_ref[:, cols]


def join_kernel(toks, *refs):
    zs_refs, kv_ref, qc_ref = refs[:GROUP], refs[GROUP], refs[GROUP + 1]
    _, _, _, z = place()
    for step in range(GROUP):
        src = lax.rem(z + GROUP - step, GROUP)
        kv_ref[pl.ds(pl.multiple_of(src * toks, toks), toks), :] = zs_refs[step][:toks, :]
        rows = PIECES * CAP
        qc_ref[pl.ds(pl.multiple_of(src * rows, rows), rows), :] = zs_refs[step][toks:, :]


def side_first(x, y, m, ctoks):
    return (lax.rem(x + XS - m, XS) * SIDES + y) * ctoks


def pick_kernel(ctoks, pos_ref, *refs):
    kv_refs, out_ref = refs[:XS], refs[XS]
    _, x, y, _ = place()
    pos_row = pos_ref[...]
    glob = pos_row.shape[1]
    pos_col = column(pos_row)
    got = jnp.zeros((glob, KV), F32)
    for m in range(XS):
        first = side_first(x, y, m, ctoks)
        got = got + dot_nn(hot(pos_col == first + iota((glob, ctoks), 1)), kv_refs[m][...])
    out_ref[:glob, :] = got.astype(BF16)
    end = slice(ctoks - BLOCK, ctoks)
    out_ref[glob : glob + BLOCK, :] = jnp.where(y == 0, kv_refs[0][end, :], kv_refs[1][end, :])
    out_ref[glob + BLOCK : glob + 2 * BLOCK, :] = jnp.where(
        y == 0, kv_refs[3][:BLOCK, :], kv_refs[0][:BLOCK, :]
    )


def fill_slots(y, slots, mine_ref, peer_ref):
    half = GROUP * CAP
    rows = PIECES * CAP
    for ref, side in ((mine_ref, y), (peer_ref, 1 - y)):
        for d in range(GROUP):
            at = pl.ds(pl.multiple_of(side * half + d * CAP, CAP), CAP)
            for p in range(PIECES):
                begin = d * rows + p * CAP
                slots[at, p * KV : (p + 1) * KV] = ref[begin : begin + CAP, :]


def padded_ranks(x, toks, pos_col, before):
    lane = iota((1, 2 * GROUP * CAP), 1)
    dev = x * (SIDES * GROUP) + lane // CAP
    start = jnp.sum((pos_col < dev * toks).astype(F32), axis=0, keepdims=True).astype(jnp.int32)
    stop = jnp.sum((pos_col < (dev + 1) * toks).astype(F32), axis=0, keepdims=True).astype(jnp.int32)
    rank = start + lax.rem(lane, CAP)
    return jnp.where(rank < stop, rank - before, -1)


def chunk_rows(slots, ranks, base):
    pick = hot(ranks == base + iota((CHUNK, ranks.shape[1]), 0))
    got = dot_nn(pick, slots[...]).astype(BF16)
    q = jnp.concatenate([got[:, h * DH : (h + 1) * DH] for h in range(REP)], axis=0)
    g = jnp.concatenate([got[:, WIDE + h * DH : WIDE + (h + 1) * DH] for h in range(REP)], axis=0)
    return q, g


def stats_kernel(toks, pos_ref, *refs):
    kv_refs, mine_ref, peer_ref, out_ref = refs[:XS], refs[XS], refs[XS + 1], refs[XS + 2]
    slots, sc = refs[XS + 3 :]
    _, x, y, _ = place()
    pos_row = pos_ref[...]
    before = below(pos_row, x * (SIDES * GROUP * toks))
    fill_slots(y, slots, mine_ref, peer_ref)
    ranks = padded_ranks(x, toks, column(pos_row), before)
    ctoks = GROUP * toks
    out_ref[...] = jnp.zeros_like(out_ref)

    def chunk(ch, carry):
        q, g = chunk_rows(slots, ranks, ch * CHUNK)
        top = jnp.full((1, GROWS), NEG, F32)
        for m in range(XS):
            s = dot_nt(kv_refs[m][:, :DH], q)
            sc[m * ctoks : (m + 1) * ctoks, :] = s
            top = jnp.maximum(top, jnp.max(s, axis=0, keepdims=True))
        total = jnp.zeros((1, GROWS), F32)
        dsum = jnp.zeros((1, GROWS), F32)
        for m in range(XS):
            w = jnp.exp2((sc[m * ctoks : (m + 1) * ctoks, :] - top) * EXP2)
            total = total + jnp.sum(w, axis=0, keepdims=True)
            dsum = dsum + jnp.sum(w * dot_nt(kv_refs[m][:, DH:], g), axis=0, keepdims=True)
        out_ref[ch, 0:1, :] = top
        out_ref[ch, 1:2, :] = total
        out_ref[ch, 2:3, :] = dsum
        return carry

    lax.fori_loop(0, (pair_count(pos_row, x, toks) + CHUNK - 1) // CHUNK, chunk, 0)


def near_kernel(seq, toks, pos_ref, after_ref, kv_ref, e2_ref, e2p_ref, *refs):
    qg_in = refs[:GROUP]
    outs = refs[GROUP : 2 * GROUP]
    dw_ref, dkg_ref, e5_ref, win, dwin, kg, kgt, qg, out = refs[2 * GROUP :]
    me, _, _, z = place()
    ctoks = GROUP * toks
    pos_row = pos_ref[...]
    glob = pos_row.shape[1]
    pos_col = column(pos_row)
    first = (me // GROUP) * ctoks
    win[:BLOCK, :] = e2p_ref[glob : glob + BLOCK, :]
    win[BLOCK : BLOCK + ctoks, :] = kv_ref[...]
    win[BLOCK + ctoks :, :] = e2p_ref[glob + BLOCK :, :]
    both = (e2_ref[:glob, :].astype(F32) + e2p_ref[:glob, :].astype(F32)).astype(BF16)
    kg[...] = both
    kgt[...] = both.T
    for step in range(GROUP):
        src = lax.rem(z + GROUP - step, GROUP)
        qg[pl.ds(pl.multiple_of(src * toks, toks), toks), :] = qg_in[step][...]
    dwin[...] = jnp.zeros_like(dwin)
    dkg_ref[...] = jnp.zeros_like(dkg_ref)

    def block(b, carry):
        base = first + b * BLOCK
        here = pl.ds(pl.multiple_of(b * BLOCK, BLOCK), 3 * BLOCK)
        mine = pl.ds(pl.multiple_of(b * BLOCK, BLOCK), BLOCK)
        kn, vn = win[here, :DH], win[here, DH:]
        q = jnp.concatenate([qg[mine, h * DH : (h + 1) * DH] for h in range(REP)], axis=0)
        g = jnp.concatenate([qg[mine, WIDE + h * DH : WIDE + (h + 1) * DH] for h in range(REP)], axis=0)
        key_tok = base - BLOCK + iota((3 * BLOCK, 1), 0)
        key_glob = jnp.sum((key_tok == pos_row).astype(F32), axis=1, keepdims=True)
        usable = (key_tok >= 0) & (key_tok < seq) & (key_glob < 0.5)
        row_tok = base + lax.rem(iota((1, ROWS), 1), BLOCK)
        live = 1.0 - jnp.sum((pos_col == row_tok).astype(F32), axis=0, keepdims=True)

        sn = jnp.where(usable, dot_nt(kn, q), NEG)
        sf = dot_nt(kg[:, :DH], q)
        top = jnp.maximum(jnp.max(sn, axis=0, keepdims=True), jnp.max(sf, axis=0, keepdims=True))
        wn = jnp.exp2((sn - top) * EXP2)
        wf = jnp.exp2((sf - top) * EXP2)
        dn = dot_nt(vn, g)
        df = dot_nt(kg[:, DH:], g)
        total = jnp.sum(wn, axis=0, keepdims=True) + jnp.sum(wf, axis=0, keepdims=True)
        dsum = jnp.sum(wn * dn, axis=0, keepdims=True) + jnp.sum(wf * df, axis=0, keepdims=True)
        inv = 1.0 / total
        delta = dsum * inv
        mixed = (dot_nn(vn.T, wn.astype(BF16)) + dot_nn(kgt[DH:, :], wf.astype(BF16))) * inv
        inv_live = inv * live
        pn = wn * inv_live
        pf = wf * inv_live
        dsn = (pn * (dn - delta)).astype(BF16)
        dsf = (pf * (df - delta)).astype(BF16)
        gq = (dot_nn(kn.T, dsn) + dot_nn(kgt[:DH, :], dsf)) * SCALE
        dwin[here, :DH] += dot_nn(dsn, q) * SCALE
        dwin[here, DH:] += dot_nn(pn.astype(BF16), g)
        dkg_ref[:, :DH] += dot_nn(dsf, q) * SCALE
        dkg_ref[:, DH:] += dot_nn(pf.astype(BF16), g)
        att = mixed.T.astype(BF16)
        gqr = gq.T.astype(BF16)
        for h in range(REP):
            rows = slice(h * BLOCK, (h + 1) * BLOCK)
            out[mine, h * DH : (h + 1) * DH] = att[rows]
            out[mine, WIDE + h * DH : WIDE + (h + 1) * DH] = gqr[rows]
        return carry

    lax.fori_loop(0, ctoks // BLOCK, block, 0, unroll=4)
    for step in range(GROUP):
        dst = lax.rem(z + step, GROUP)
        outs[step][...] = out[pl.ds(pl.multiple_of(dst * toks, toks), toks), :]
    dw_ref[...] = dwin[BLOCK : BLOCK + ctoks, :]
    e5_ref[:glob, :] = dkg_ref[...].astype(BF16)
    e5_ref[glob : glob + BLOCK, :] = dwin[:BLOCK, :].astype(BF16)
    e5_ref[glob + BLOCK :, :] = dwin[BLOCK + ctoks :, :].astype(BF16)


def grads_kernel(toks, pos_ref, *refs):
    kv_refs, refs = refs[:XS], refs[XS:]
    mine_ref, peer_ref, st_ref, stp_ref, dw_ref, dkg_ref = refs[:6]
    dkv, e4_ref, keep_ref, slots, kvt, rows_out = refs[6:]
    _, x, y, _ = place()
    ctoks = GROUP * toks
    pos_row = pos_ref[...]
    glob = pos_row.shape[1]
    pos_col = column(pos_row)
    pair_first = x * (SIDES * ctoks)
    before = below(pos_row, pair_first)
    count = pair_count(pos_row, x, toks)
    fill_slots(y, slots, mine_ref, peer_ref)
    ranks = padded_ranks(x, toks, pos_col, before)
    rows_out[...] = jnp.zeros_like(rows_out)
    for m in range(XS):
        kvt[m] = kv_refs[m][...].T

    far_high, far_low = split(dkg_ref[...])
    for m in range(XS):
        first = side_first(x, y, m, ctoks)
        mask = hot(first + iota((ctoks, glob), 0) == pos_row)
        whole = dot_nn(mask, far_high) + dot_nn(mask, far_low)
        dkv[m] = whole + dw_ref[...] if m == 0 else whole

    def chunk(ch, carry):
        base = ch * CHUNK
        q, g = chunk_rows(slots, ranks, base)
        valid = (base + lax.rem(iota((1, GROWS), 1), CHUNK) < count).astype(F32)
        here, there = st_ref[ch], stp_ref[ch]
        top = jnp.maximum(here[0:1], there[0:1])
        a = jnp.exp2((here[0:1] - top) * EXP2)
        b = jnp.exp2((there[0:1] - top) * EXP2)
        inv = 1.0 / (here[1:2] * a + there[1:2] * b)
        delta = (here[2:3] * a + there[2:3] * b) * inv
        inv = inv * valid
        att = jnp.zeros((DH, GROWS), F32)
        gq = jnp.zeros((DH, GROWS), F32)
        for m in range(XS):
            p = jnp.exp2((dot_nt(kv_refs[m][:, :DH], q) - top) * EXP2) * inv
            p_high, p_low = split(p)
            ds = (p * (dot_nt(kv_refs[m][:, DH:], g) - delta)).astype(BF16)
            dkv[m, :, :DH] += dot_nn(ds, q) * SCALE
            dkv[m, :, DH:] += dot_nn(p_high, g)
            vt = kvt[m, DH:, :]
            att = att + dot_nn(vt, p_high) + dot_nn(vt, p_low)
            gq = gq + dot_nn(kvt[m, :DH, :], ds)
        att = att.T
        gq = (gq * SCALE).T
        rows = pl.ds(pl.multiple_of(base, CHUNK), CHUNK)
        for h in range(REP):
            part = slice(h * CHUNK, (h + 1) * CHUNK)
            rows_out[rows, h * DH : (h + 1) * DH] = att[part]
            rows_out[rows, WIDE + h * DH : WIDE + (h + 1) * DH] = gq[part]
        return carry

    lax.fori_loop(0, (count + CHUNK - 1) // CHUNK, chunk, 0)
    part_high, part_low = split(rows_out[...])
    slot = iota((GROUP * CAP, 2 * GROUP * CAP), 0)
    lane = iota((GROUP * CAP, 2 * GROUP * CAP), 1)

    def cluster_mask(side):
        begin = below(pos_row, pair_first + side * ctoks) - before
        size = below(pos_row, pair_first + (side + 1) * ctoks) - before - begin
        return hot((lane == begin + slot) & (slot < size))

    e4_ref[...] = dot_nn(cluster_mask(1 - y), part_high).astype(BF16)
    mask = cluster_mask(y)
    keep_ref[...] = dot_nn(mask, part_high) + dot_nn(mask, part_low)


def peer_kernel(toks, pos_ref, dkv_ref, e5p_ref, own_ref, *send_refs):
    _, x, y, _ = place()
    ctoks = GROUP * toks
    pos_row = pos_ref[...]
    glob = pos_row.shape[1]
    far = e5p_ref[:glob, :]
    low = e5p_ref[glob : glob + BLOCK, :].astype(F32)
    high = e5p_ref[glob + BLOCK :, :].astype(F32)
    at_zero = (y == 0).astype(F32)
    at_one = 1.0 - at_zero
    none = jnp.zeros((ctoks - BLOCK, KV), F32)
    edges = {
        0: jnp.concatenate([high * at_one, none[BLOCK:], low * at_zero], axis=0),
        1: jnp.concatenate([none, low * at_one], axis=0),
        3: jnp.concatenate([high * at_zero, none], axis=0),
    }
    for m in range(XS):
        first = side_first(x, y, m, ctoks)
        mask = hot(first + iota((ctoks, glob), 0) == pos_row)
        whole = dkv_ref[m] + dot_nn(mask, far)
        if m in edges:
            whole = whole + edges[m]
        if m == 0:
            own_ref[...] = whole
        else:
            send_refs[XS - m - 1][...] = whole.astype(BF16)


def merge_kernel(toks, pos_ref, own_ref, *refs):
    got_refs, refs = refs[: XS - 1], refs[XS - 1 :]
    keep_ref, e4p_ref = refs[0], refs[1]
    zs_refs, whole = refs[2 : 2 + GROUP], refs[2 + GROUP]
    me, _, _, z = place()
    pos_row = pos_ref[...]
    total = own_ref[...]
    for ref in got_refs:
        total = total + ref[...].astype(F32)
    whole[...] = total.astype(BF16)
    rows = (keep_ref[...] + e4p_ref[...].astype(F32)).astype(BF16)
    first_dev = (me // GROUP) * GROUP
    before = below(pos_row, first_dev * toks)
    slot = iota((CAP, GROUP * CAP), 0)
    lane = iota((CAP, GROUP * CAP), 1)
    for step in range(GROUP):
        j = lax.rem(z + step, GROUP)
        zs_refs[step][:toks, :] = whole[pl.ds(pl.multiple_of(j * toks, toks), toks), :]
        begin = below(pos_row, (first_dev + j) * toks) - before
        size = below(pos_row, (first_dev + j + 1) * toks) - before - begin
        got = dot_nn(hot((lane == begin + slot) & (slot < size)), rows).astype(BF16)
        for p in range(PIECES):
            zs_refs[step][toks + CAP * p : toks + CAP * (p + 1), :] = got[:, p * KV : (p + 1) * KV]


def post_kernel(toks, pos_ref, *refs):
    zs_refs, o_refs = refs[:GROUP], refs[GROUP : 2 * GROUP]
    att_ref, gq_ref, dk_ref, dv_ref = refs[2 * GROUP :]
    me, _, _, z = place()
    pos_row = pos_ref[...]
    first = me * toks
    slot = slots_along_rows(pos_row, first + iota((toks, 1), 0), below(pos_row, first))
    mask = hot(slot == iota((toks, CAP), 1))
    is_glob = slot >= 0
    for step in range(GROUP):
        j = lax.rem(z + GROUP - step, GROUP)
        head = pl.ds(pl.multiple_of(j * DH, DH), DH)
        dk_ref[:, head] = zs_refs[step][:toks, :DH]
        dv_ref[:, head] = zs_refs[step][:toks, DH:]
        for p in range(PIECES):
            rows = zs_refs[step][toks + CAP * p : toks + CAP * (p + 1), :]
            placed = dot_nn(mask, rows)
            here = o_refs[step][:, p * KV : (p + 1) * KV].astype(F32)
            value = jnp.where(is_glob, placed, here).astype(BF16)
            ref, off = (att_ref, p * KV) if p * KV < WIDE else (gq_ref, p * KV - WIDE)
            ref[:, pl.ds(pl.multiple_of(j * WIDE + off, KV), KV)] = value


VM = pl.BlockSpec(memory_space=pltpu.VMEM)
HBM = pl.BlockSpec(memory_space=pltpu.HBM)


def call(kernel, outs, args, scratch=(), specs=None, sems=0, flops=0, moved=0):
    return pl.pallas_call(
        kernel,
        out_shape=tuple(jax.ShapeDtypeStruct(s, d) for s, d in outs),
        in_specs=specs or [VM] * len(args),
        out_specs=(VM,) * len(outs),
        scratch_shapes=[pltpu.VMEM(s, d) for s, d in scratch] + [pltpu.SemaphoreType.DMA((sems,))] * (sems > 0),
        compiler_params=pltpu.CompilerParams(vmem_limit_bytes=40 * 1024 * 1024),
        cost_estimate=pl.CostEstimate(flops=flops, bytes_accessed=moved, transcendentals=0),
    )(*args)


def local(queries, keys, values, grad_out, positions):
    toks, width = queries.shape
    kwidth = keys.shape[1]
    devices = lax.axis_size("ctx")
    seq = toks * devices
    ctoks = GROUP * toks
    glob = positions.shape[0]
    zrows = toks + PIECES * CAP
    part = ((toks, 2 * WIDE), BF16)
    zpart = ((zrows, KV), BF16)
    cpart = ((ctoks, KV), BF16)
    ppart = ((glob + 2 * BLOCK, KV), BF16)

    def zperm(a, step):
        pairs = [(c, c // GROUP * GROUP + (c + step) % GROUP) for c in range(devices)]
        return lax.ppermute(a, "ctx", pairs)

    def xperm(a, step):
        return lax.ppermute(a, "ctx", [(c, (c + step * SIDES * GROUP) % devices) for c in range(devices)])

    def yperm(a):
        return lax.ppermute(a, "ctx", [(c, c ^ GROUP) for c in range(devices)])

    sent = call(
        functools.partial(prep_kernel, toks),
        [zpart] * GROUP + [part] * GROUP + [((1, glob), jnp.int32)],
        tuple(pltpu.with_memory_space_constraint(a, pltpu.HBM) for a in (positions.reshape(1, glob), queries, keys, values, grad_out)),
        scratch=[
            ((CAP, 2 * width), BF16),
            ((1, glob), jnp.int32),
            ((toks, width), BF16),
            ((toks, width), BF16),
            ((toks, kwidth), BF16),
            ((toks, kwidth), BF16),
        ],
        specs=[HBM] * 5,
        sems=5,
        moved=4 << 20,
    )
    pos = sent[2 * GROUP]
    zs = [sent[0]] + [zperm(sent[step], step) for step in range(1, GROUP)]
    kv0, qc = call(
        functools.partial(join_kernel, toks), [cpart, ((GROUP * PIECES * CAP, KV), BF16)], tuple(zs), moved=1 << 20
    )
    kvs = [kv0] + [xperm(kv0, m) for m in range(1, XS)]
    qcp = yperm(qc)
    qgs = [sent[GROUP]] + [zperm(sent[GROUP + step], step) for step in range(1, GROUP)]
    (e2,) = call(functools.partial(pick_kernel, ctoks), [ppart], (pos, *kvs), moved=6 << 20)
    e2p = yperm(e2)
    (st,) = call(
        functools.partial(stats_kernel, toks),
        [((glob // CHUNK, 8, GROWS), F32)],
        (pos, *kvs, qc, qcp),
        scratch=[((2 * GROUP * CAP, 2 * WIDE), BF16), ((XS * ctoks, GROWS), F32)],
        moved=14 << 20,
    )
    stp = yperm(st)
    *outs, dw, dkg, e5 = call(
        functools.partial(near_kernel, seq, toks),
        [part] * GROUP + [((ctoks, KV), F32), ((glob, KV), F32), ppart],
        (pos, st, kv0, e2, e2p, *qgs),
        scratch=[
            ((ctoks + 2 * BLOCK, KV), BF16),
            ((ctoks + 2 * BLOCK, KV), F32),
            ((glob, KV), BF16),
            ((KV, glob), BF16),
            ((ctoks, 2 * WIDE), BF16),
            ((ctoks, 2 * WIDE), BF16),
        ],
        moved=40 << 20,
    )
    e5p = yperm(e5)
    os = [outs[0]] + [zperm(outs[step], step) for step in range(1, GROUP)]
    dkv, e4, keep = call(
        functools.partial(grads_kernel, toks),
        [((XS, ctoks, KV), F32), ((GROUP * CAP, 2 * WIDE), BF16), ((GROUP * CAP, 2 * WIDE), F32)],
        (pos, *kvs, qc, qcp, st, stp, dw, dkg),
        scratch=[
            ((2 * GROUP * CAP, 2 * WIDE), BF16),
            ((XS, KV, ctoks), BF16),
            ((2 * GROUP * CAP, 2 * WIDE), F32),
        ],
        moved=24 << 20,
    )
    own, *sends = call(
        functools.partial(peer_kernel, toks),
        [((ctoks, KV), F32)] + [cpart] * (XS - 1),
        (pos, dkv, e5p),
        moved=3 << 20,
    )
    got = [xperm(sends[m - 1], m) for m in range(1, XS)]
    e4p = yperm(e4)
    zback = call(
        functools.partial(merge_kernel, toks),
        [zpart] * GROUP,
        (pos, own, *got, keep, e4p),
        scratch=[((ctoks, KV), BF16)],
        moved=3 << 20,
    )
    zr = [zback[0]] + [zperm(zback[step], step) for step in range(1, GROUP)]
    return call(
        functools.partial(post_kernel, toks),
        [((toks, width), BF16)] * 2 + [((toks, kwidth), BF16)] * 2,
        (pos, *zr, *os),
        moved=4 << 20,
    )


def solution(mesh):
    rows = P(("dp", "ctx"), None)
    return jax.shard_map(
        local,
        mesh=mesh,
        in_specs=(rows, rows, rows, rows, P("dp")),
        out_specs=(rows, rows, rows, rows),
        check_vma=False,
    )
```

```python
import functools
import math

import jax
import jax.numpy as jnp
from jax import lax
from jax.experimental import pallas as pl
from jax.experimental.pallas import tpu as pltpu
from jax.sharding import PartitionSpec as P


HQ = 16
HK = 4
DH = 128
BLOCK = 64
CAP = 32
REP = HQ // HK
GROUP = 4
SIDES = 2
XS = 4
CHUNK = 128
ROWS = REP * BLOCK
GROWS = REP * CHUNK
WIDE = REP * DH
KV = 2 * DH
PIECES = 2 * WIDE // KV
EDGE = BLOCK // PIECES
SCALE = 1.0 / math.sqrt(DH)
EXP2 = SCALE * math.log2(math.e)
NEG = -1e30

F32 = jnp.float32
BF16 = jnp.bfloat16


def dot_nt(a, b):
    return lax.dot_general(a, b, (((1,), (1,)), ((), ())), preferred_element_type=F32)


def dot_nn(a, b):
    return lax.dot_general(a, b, (((1,), (0,)), ((), ())), preferred_element_type=F32)


def iota(shape, dim):
    return lax.broadcasted_iota(jnp.int32, shape, dim)


def hot(mask):
    return mask.astype(F32).astype(BF16)


def split(x):
    high = x.astype(BF16)
    return high, (x - high.astype(F32)).astype(BF16)


def place():
    me = lax.axis_index("ctx")
    cluster = me // GROUP
    return me, cluster // SIDES, lax.rem(cluster, SIDES), lax.rem(me, GROUP)


def column(row):
    n = row.shape[1]
    eye = iota((n, n), 0) == iota((n, n), 1)
    wide = jnp.where(eye, jnp.broadcast_to(row, (n, n)), 0).astype(F32)
    return jnp.sum(wide, axis=1, keepdims=True).astype(jnp.int32)


def below(pos_row, edge):
    return jnp.sum((pos_row < edge).astype(F32), axis=1, keepdims=True).astype(jnp.int32)


def pair_count(pos_row, x, toks):
    size = SIDES * GROUP * toks
    inside = (pos_row >= x * size) & (pos_row < (x + 1) * size)
    return jnp.sum(inside.astype(F32)).astype(jnp.int32)


def slots_along_lanes(pos_col, tok_row, before):
    is_row = jnp.sum((pos_col == tok_row).astype(F32), axis=0, keepdims=True)
    rank = jnp.sum((pos_col < tok_row).astype(F32), axis=0, keepdims=True).astype(jnp.int32)
    return jnp.where(is_row > 0.5, rank - before, -1)


def slots_along_rows(pos_row, tok_col, before):
    is_col = jnp.sum((pos_row == tok_col).astype(F32), axis=1, keepdims=True)
    rank = jnp.sum((pos_row < tok_col).astype(F32), axis=1, keepdims=True).astype(jnp.int32)
    return jnp.where(is_col > 0.5, rank - before, -1)


def prep_kernel(toks, pos_any, q_any, k_any, v_any, g_any, *refs):
    zs_refs, qg_refs, pos_out = refs[:GROUP], refs[GROUP : 2 * GROUP], refs[2 * GROUP]
    picked, pos_ref, q_ref, g_ref, k_ref, v_ref, sems = refs[2 * GROUP + 1 :]
    pos_copy = pltpu.make_async_copy(pos_any, pos_ref, sems.at[4])
    pos_copy.start()
    copies = [
        pltpu.make_async_copy(src, dst, sems.at[i])
        for i, (src, dst) in enumerate(((q_any, q_ref), (g_any, g_ref), (k_any, k_ref), (v_any, v_ref)))
    ]
    for copy in copies:
        copy.start()
    me, _, _, z = place()
    pos_copy.wait()
    pos_row = pos_ref[...]
    pos_out[...] = pos_row
    first = me * toks
    slot = slots_along_lanes(column(pos_row), first + iota((1, toks), 1), below(pos_row, first))
    pick = hot(slot == iota((CAP, toks), 0))
    width = HQ * DH
    for copy in copies:
        copy.wait()
    picked[:, :width] = dot_nn(pick, q_ref[...]).astype(BF16)
    picked[:, width:] = dot_nn(pick, g_ref[...]).astype(BF16)
    for step in range(GROUP):
        j = lax.rem(z + step, GROUP)
        head = pl.ds(pl.multiple_of(j * DH, DH), DH)
        cols = pl.ds(pl.multiple_of(j * WIDE, WIDE), WIDE)
        zs_refs[step][:toks, :DH] = k_ref[:, head]
        zs_refs[step][:toks, DH:] = v_ref[:, head]
        for p in range(PIECES):
            base = j * WIDE + p * KV if p * KV < WIDE else width + j * WIDE + p * KV - WIDE
            part = picked[:, pl.ds(pl.multiple_of(base, KV), KV)]
            zs_refs[step][toks + CAP * p : toks + CAP * (p + 1), :] = part
        qg_refs[step][:, :WIDE] = q_ref[:, cols]
        qg_refs[step][:, WIDE:] = g_ref[:, cols]


def join_kernel(toks, *refs):
    zs_refs, kv_ref, qc_ref = refs[:GROUP], refs[GROUP], refs[GROUP + 1]
    _, _, y, z = place()
    for step in range(GROUP):
        src = lax.rem(z + GROUP - step, GROUP)
        kv_ref[pl.ds(pl.multiple_of(src * toks, toks), toks), :] = zs_refs[step][:toks, :]
        rows = PIECES * CAP
        qc_ref[pl.ds(pl.multiple_of(src * rows, rows), rows), :] = zs_refs[step][toks:, :]
    last = slice((GROUP * toks) - BLOCK, GROUP * toks)
    qc_ref[GROUP * PIECES * CAP :, :] = jnp.where(y == 0, kv_ref[last, :], kv_ref[:BLOCK, :])


def side_first(x, y, m, ctoks):
    return (lax.rem(x + XS - m, XS) * SIDES + y) * ctoks


def pick_kernel(ctoks, pos_ref, *refs):
    kv_refs, out_ref = refs[:XS], refs[XS]
    _, x, y, _ = place()
    pos_row = pos_ref[...]
    glob = pos_row.shape[1]
    pos_col = column(pos_row)
    got = jnp.zeros((glob, KV), F32)
    for m in range(XS):
        first = side_first(x, y, m, ctoks)
        got = got + dot_nn(hot(pos_col == first + iota((glob, ctoks), 1)), kv_refs[m][...])
    out_ref[:glob, :] = got.astype(BF16)
    end = slice(ctoks - BLOCK, ctoks)
    out_ref[glob:, :] = jnp.where(y == 0, kv_refs[3][:BLOCK, :], kv_refs[1][end, :])


def fill_slots(y, slots, mine_ref, peer_ref):
    half = GROUP * CAP
    rows = PIECES * CAP
    for ref, side in ((mine_ref, y), (peer_ref, 1 - y)):
        for d in range(GROUP):
            at = pl.ds(pl.multiple_of(side * half + d * CAP, CAP), CAP)
            for p in range(PIECES):
                begin = d * rows + p * CAP
                slots[at, p * KV : (p + 1) * KV] = ref[begin : begin + CAP, :]


def padded_ranks(x, toks, pos_col, before):
    lane = iota((1, 2 * GROUP * CAP), 1)
    dev = x * (SIDES * GROUP) + lane // CAP
    start = jnp.sum((pos_col < dev * toks).astype(F32), axis=0, keepdims=True).astype(jnp.int32)
    stop = jnp.sum((pos_col < (dev + 1) * toks).astype(F32), axis=0, keepdims=True).astype(jnp.int32)
    rank = start + lax.rem(lane, CAP)
    return jnp.where(rank < stop, rank - before, -1)


def chunk_rows(slots, ranks, base):
    pick = hot(ranks == base + iota((CHUNK, ranks.shape[1]), 0))
    got = dot_nn(pick, slots[...]).astype(BF16)
    q = jnp.concatenate([got[:, h * DH : (h + 1) * DH] for h in range(REP)], axis=0)
    g = jnp.concatenate([got[:, WIDE + h * DH : WIDE + (h + 1) * DH] for h in range(REP)], axis=0)
    return q, g


def stats_kernel(toks, pos_ref, *refs):
    kv_refs, mine_ref, peer_ref, out_ref = refs[:XS], refs[XS], refs[XS + 1], refs[XS + 2]
    slots, sc = refs[XS + 3 :]
    _, x, y, _ = place()
    pos_row = pos_ref[...]
    before = below(pos_row, x * (SIDES * GROUP * toks))
    fill_slots(y, slots, mine_ref, peer_ref)
    ranks = padded_ranks(x, toks, column(pos_row), before)
    ctoks = GROUP * toks
    out_ref[...] = jnp.zeros_like(out_ref)

    def chunk(ch, carry):
        q, g = chunk_rows(slots, ranks, ch * CHUNK)
        top = jnp.full((1, GROWS), NEG, F32)
        for m in range(XS):
            s = dot_nt(kv_refs[m][:, :DH], q)
            sc[m * ctoks : (m + 1) * ctoks, :] = s
            top = jnp.maximum(top, jnp.max(s, axis=0, keepdims=True))
        total = jnp.zeros((1, GROWS), F32)
        dsum = jnp.zeros((1, GROWS), F32)
        for m in range(XS):
            w = jnp.exp2((sc[m * ctoks : (m + 1) * ctoks, :] - top) * EXP2)
            total = total + jnp.sum(w, axis=0, keepdims=True)
            dsum = dsum + jnp.sum(w * dot_nt(kv_refs[m][:, DH:], g), axis=0, keepdims=True)
        out_ref[ch, 0:1, :] = top
        out_ref[ch, 1:2, :] = total
        out_ref[ch, 2:3, :] = dsum
        return carry

    lax.fori_loop(0, (pair_count(pos_row, x, toks) + CHUNK - 1) // CHUNK, chunk, 0)


def near_kernel(seq, toks, pos_ref, after_ref, kv_ref, e2_ref, e2p_ref, qcp_ref, *refs):
    qg_in = refs[:GROUP]
    outs = refs[GROUP : 2 * GROUP]
    dw_ref, dkg_ref, e5_ref, edge_ref, win, dwin, kg, kgt, qg, out = refs[2 * GROUP :]
    me, _, y, z = place()
    ctoks = GROUP * toks
    pos_row = pos_ref[...]
    glob = pos_row.shape[1]
    pos_col = column(pos_row)
    first = (me // GROUP) * ctoks
    far_edge = e2p_ref[glob:, :]
    near_edge = qcp_ref[GROUP * PIECES * CAP :, :]
    win[:BLOCK, :] = jnp.where(y == 0, far_edge, near_edge)
    win[BLOCK : BLOCK + ctoks, :] = kv_ref[...]
    win[BLOCK + ctoks :, :] = jnp.where(y == 0, near_edge, far_edge)
    both = (e2_ref[:glob, :].astype(F32) + e2p_ref[:glob, :].astype(F32)).astype(BF16)
    kg[...] = both
    kgt[...] = both.T
    for step in range(GROUP):
        src = lax.rem(z + GROUP - step, GROUP)
        qg[pl.ds(pl.multiple_of(src * toks, toks), toks), :] = qg_in[step][...]
    dwin[...] = jnp.zeros_like(dwin)
    dkg_ref[...] = jnp.zeros_like(dkg_ref)

    def block(b, carry):
        base = first + b * BLOCK
        here = pl.ds(pl.multiple_of(b * BLOCK, BLOCK), 3 * BLOCK)
        mine = pl.ds(pl.multiple_of(b * BLOCK, BLOCK), BLOCK)
        kn, vn = win[here, :DH], win[here, DH:]
        q = jnp.concatenate([qg[mine, h * DH : (h + 1) * DH] for h in range(REP)], axis=0)
        g = jnp.concatenate([qg[mine, WIDE + h * DH : WIDE + (h + 1) * DH] for h in range(REP)], axis=0)
        key_tok = base - BLOCK + iota((3 * BLOCK, 1), 0)
        key_glob = jnp.sum((key_tok == pos_row).astype(F32), axis=1, keepdims=True)
        usable = (key_tok >= 0) & (key_tok < seq) & (key_glob < 0.5)
        row_tok = base + lax.rem(iota((1, ROWS), 1), BLOCK)
        live = 1.0 - jnp.sum((pos_col == row_tok).astype(F32), axis=0, keepdims=True)

        sn = jnp.where(usable, dot_nt(kn, q), NEG)
        sf = dot_nt(kg[:, :DH], q)
        top = jnp.maximum(jnp.max(sn, axis=0, keepdims=True), jnp.max(sf, axis=0, keepdims=True))
        wn = jnp.exp2((sn - top) * EXP2)
        wf = jnp.exp2((sf - top) * EXP2)
        dn = dot_nt(vn, g)
        df = dot_nt(kg[:, DH:], g)
        total = jnp.sum(wn, axis=0, keepdims=True) + jnp.sum(wf, axis=0, keepdims=True)
        dsum = jnp.sum(wn * dn, axis=0, keepdims=True) + jnp.sum(wf * df, axis=0, keepdims=True)
        inv = 1.0 / total
        delta = dsum * inv
        mixed = (dot_nn(vn.T, wn.astype(BF16)) + dot_nn(kgt[DH:, :], wf.astype(BF16))) * inv
        inv_live = inv * live
        pn = wn * inv_live
        pf = wf * inv_live
        dsn = (pn * (dn - delta)).astype(BF16)
        dsf = (pf * (df - delta)).astype(BF16)
        gq = (dot_nn(kn.T, dsn) + dot_nn(kgt[:DH, :], dsf)) * SCALE
        dwin[here, :DH] += dot_nn(dsn, q) * SCALE
        dwin[here, DH:] += dot_nn(pn.astype(BF16), g)
        dkg_ref[:, :DH] += dot_nn(dsf, q) * SCALE
        dkg_ref[:, DH:] += dot_nn(pf.astype(BF16), g)
        att = mixed.T.astype(BF16)
        gqr = gq.T.astype(BF16)
        for h in range(REP):
            rows = slice(h * BLOCK, (h + 1) * BLOCK)
            out[mine, h * DH : (h + 1) * DH] = att[rows]
            out[mine, WIDE + h * DH : WIDE + (h + 1) * DH] = gqr[rows]
        return carry

    lax.fori_loop(0, ctoks // BLOCK, block, 0, unroll=4)
    for step in range(GROUP):
        dst = lax.rem(z + step, GROUP)
        outs[step][...] = out[pl.ds(pl.multiple_of(dst * toks, toks), toks), :]
    dw_ref[...] = dwin[BLOCK : BLOCK + ctoks, :]
    e5_ref[:glob, :] = dkg_ref[...].astype(BF16)
    low, high = dwin[:BLOCK, :], dwin[BLOCK + ctoks :, :]
    e5_ref[glob:, :] = jnp.where(y == 0, low, high).astype(BF16)
    edge_ref[...] = jnp.where(y == 0, high, low).astype(BF16)


def grads_kernel(toks, pos_ref, *refs):
    kv_refs, refs = refs[:XS], refs[XS:]
    mine_ref, peer_ref, st_ref, stp_ref, dw_ref, dkg_ref, edge_ref = refs[:7]
    dkv, e4_ref, keep_ref, slots, kvt, rows_out = refs[7:]
    _, x, y, _ = place()
    ctoks = GROUP * toks
    pos_row = pos_ref[...]
    glob = pos_row.shape[1]
    pos_col = column(pos_row)
    pair_first = x * (SIDES * ctoks)
    before = below(pos_row, pair_first)
    count = pair_count(pos_row, x, toks)
    fill_slots(y, slots, mine_ref, peer_ref)
    ranks = padded_ranks(x, toks, pos_col, before)
    rows_out[...] = jnp.zeros_like(rows_out)
    for m in range(XS):
        kvt[m] = kv_refs[m][...].T

    far_high, far_low = split(dkg_ref[...])
    for m in range(XS):
        first = side_first(x, y, m, ctoks)
        mask = hot(first + iota((ctoks, glob), 0) == pos_row)
        whole = dot_nn(mask, far_high) + dot_nn(mask, far_low)
        dkv[m] = whole + dw_ref[...] if m == 0 else whole

    def chunk(ch, carry):
        base = ch * CHUNK
        q, g = chunk_rows(slots, ranks, base)
        valid = (base + lax.rem(iota((1, GROWS), 1), CHUNK) < count).astype(F32)
        here, there = st_ref[ch], stp_ref[ch]
        top = jnp.maximum(here[0:1], there[0:1])
        a = jnp.exp2((here[0:1] - top) * EXP2)
        b = jnp.exp2((there[0:1] - top) * EXP2)
        inv = 1.0 / (here[1:2] * a + there[1:2] * b)
        delta = (here[2:3] * a + there[2:3] * b) * inv
        inv = inv * valid
        att = jnp.zeros((DH, GROWS), F32)
        gq = jnp.zeros((DH, GROWS), F32)
        for m in range(XS):
            p = jnp.exp2((dot_nt(kv_refs[m][:, :DH], q) - top) * EXP2) * inv
            p_high, p_low = split(p)
            ds = (p * (dot_nt(kv_refs[m][:, DH:], g) - delta)).astype(BF16)
            dkv[m, :, :DH] += dot_nn(ds, q) * SCALE
            dkv[m, :, DH:] += dot_nn(p_high, g)
            vt = kvt[m, DH:, :]
            att = att + dot_nn(vt, p_high) + dot_nn(vt, p_low)
            gq = gq + dot_nn(kvt[m, :DH, :], ds)
        att = att.T
        gq = (gq * SCALE).T
        rows = pl.ds(pl.multiple_of(base, CHUNK), CHUNK)
        for h in range(REP):
            part = slice(h * CHUNK, (h + 1) * CHUNK)
            rows_out[rows, h * DH : (h + 1) * DH] = att[part]
            rows_out[rows, WIDE + h * DH : WIDE + (h + 1) * DH] = gq[part]
        return carry

    lax.fori_loop(0, (count + CHUNK - 1) // CHUNK, chunk, 0)
    part_high, part_low = split(rows_out[...])
    slot = iota((GROUP * CAP, 2 * GROUP * CAP), 0)
    lane = iota((GROUP * CAP, 2 * GROUP * CAP), 1)

    def cluster_mask(side):
        begin = below(pos_row, pair_first + side * ctoks) - before
        size = below(pos_row, pair_first + (side + 1) * ctoks) - before - begin
        return hot((lane == begin + slot) & (slot < size))

    half = GROUP * CAP
    e4_ref[:half, :] = dot_nn(cluster_mask(1 - y), part_high).astype(BF16)
    for p in range(PIECES):
        e4_ref[half:, p * KV : (p + 1) * KV] = edge_ref[p * EDGE : (p + 1) * EDGE, :]
    mask = cluster_mask(y)
    keep_ref[...] = dot_nn(mask, part_high) + dot_nn(mask, part_low)


def peer_kernel(toks, pos_ref, dkv_ref, e5p_ref, own_ref, *send_refs):
    _, x, y, _ = place()
    ctoks = GROUP * toks
    pos_row = pos_ref[...]
    glob = pos_row.shape[1]
    far = e5p_ref[:glob, :]
    edge = e5p_ref[glob:, :].astype(F32)
    at_zero = (y == 0).astype(F32)
    at_one = 1.0 - at_zero
    none = jnp.zeros((ctoks - BLOCK, KV), F32)
    edges = {
        1: jnp.concatenate([none, edge * at_one], axis=0),
        3: jnp.concatenate([edge * at_zero, none], axis=0),
    }
    for m in range(XS):
        first = side_first(x, y, m, ctoks)
        mask = hot(first + iota((ctoks, glob), 0) == pos_row)
        whole = dkv_ref[m] + dot_nn(mask, far)
        if m in edges:
            whole = whole + edges[m]
        if m == 0:
            own_ref[...] = whole
        else:
            send_refs[XS - m - 1][...] = whole.astype(BF16)


def merge_kernel(toks, pos_ref, own_ref, *refs):
    got_refs, refs = refs[: XS - 1], refs[XS - 1 :]
    keep_ref, e4p_ref = refs[0], refs[1]
    zs_refs, whole = refs[2 : 2 + GROUP], refs[2 + GROUP]
    me, _, y, z = place()
    pos_row = pos_ref[...]
    total = own_ref[...]
    for ref in got_refs:
        total = total + ref[...].astype(F32)
    half = GROUP * CAP
    edge = [e4p_ref[half:, p * KV : (p + 1) * KV] for p in range(PIECES)]
    edge = jnp.concatenate(edge, axis=0).astype(F32)
    at_zero = (y == 0).astype(F32)
    none = jnp.zeros((GROUP * toks - 2 * BLOCK, KV), F32)
    total = total + jnp.concatenate([edge * (1.0 - at_zero), none, edge * at_zero], axis=0)
    whole[...] = total.astype(BF16)
    rows = (keep_ref[...] + e4p_ref[:half, :].astype(F32)).astype(BF16)
    first_dev = (me // GROUP) * GROUP
    before = below(pos_row, first_dev * toks)
    slot = iota((CAP, GROUP * CAP), 0)
    lane = iota((CAP, GROUP * CAP), 1)
    for step in range(GROUP):
        j = lax.rem(z + step, GROUP)
        zs_refs[step][:toks, :] = whole[pl.ds(pl.multiple_of(j * toks, toks), toks), :]
        begin = below(pos_row, (first_dev + j) * toks) - before
        size = below(pos_row, (first_dev + j + 1) * toks) - before - begin
        got = dot_nn(hot((lane == begin + slot) & (slot < size)), rows).astype(BF16)
        for p in range(PIECES):
            zs_refs[step][toks + CAP * p : toks + CAP * (p + 1), :] = got[:, p * KV : (p + 1) * KV]


def post_kernel(toks, pos_ref, *refs):
    zs_refs, o_refs = refs[:GROUP], refs[GROUP : 2 * GROUP]
    att_ref, gq_ref, dk_ref, dv_ref = refs[2 * GROUP :]
    me, _, _, z = place()
    pos_row = pos_ref[...]
    first = me * toks
    slot = slots_along_rows(pos_row, first + iota((toks, 1), 0), below(pos_row, first))
    mask = hot(slot == iota((toks, CAP), 1))
    is_glob = slot >= 0
    for step in range(GROUP):
        j = lax.rem(z + GROUP - step, GROUP)
        head = pl.ds(pl.multiple_of(j * DH, DH), DH)
        dk_ref[:, head] = zs_refs[step][:toks, :DH]
        dv_ref[:, head] = zs_refs[step][:toks, DH:]
        for p in range(PIECES):
            rows = zs_refs[step][toks + CAP * p : toks + CAP * (p + 1), :]
            placed = dot_nn(mask, rows)
            here = o_refs[step][:, p * KV : (p + 1) * KV].astype(F32)
            value = jnp.where(is_glob, placed, here).astype(BF16)
            ref, off = (att_ref, p * KV) if p * KV < WIDE else (gq_ref, p * KV - WIDE)
            ref[:, pl.ds(pl.multiple_of(j * WIDE + off, KV), KV)] = value


VM = pl.BlockSpec(memory_space=pltpu.VMEM)
HBM = pl.BlockSpec(memory_space=pltpu.HBM)


def call(kernel, outs, args, scratch=(), specs=None, sems=0, flops=0, moved=0):
    return pl.pallas_call(
        kernel,
        out_shape=tuple(jax.ShapeDtypeStruct(s, d) for s, d in outs),
        in_specs=specs or [VM] * len(args),
        out_specs=(VM,) * len(outs),
        scratch_shapes=[pltpu.VMEM(s, d) for s, d in scratch] + [pltpu.SemaphoreType.DMA((sems,))] * (sems > 0),
        compiler_params=pltpu.CompilerParams(vmem_limit_bytes=40 * 1024 * 1024),
        cost_estimate=pl.CostEstimate(flops=flops, bytes_accessed=moved, transcendentals=0),
    )(*args)


def local(queries, keys, values, grad_out, positions):
    toks, width = queries.shape
    kwidth = keys.shape[1]
    devices = lax.axis_size("ctx")
    seq = toks * devices
    ctoks = GROUP * toks
    glob = positions.shape[0]
    zrows = toks + PIECES * CAP
    part = ((toks, 2 * WIDE), BF16)
    zpart = ((zrows, KV), BF16)
    cpart = ((ctoks, KV), BF16)
    ppart = ((glob + BLOCK, KV), BF16)

    def zperm(a, step):
        pairs = [(c, c // GROUP * GROUP + (c + step) % GROUP) for c in range(devices)]
        return lax.ppermute(a, "ctx", pairs)

    def xperm(a, step):
        return lax.ppermute(a, "ctx", [(c, (c + step * SIDES * GROUP) % devices) for c in range(devices)])

    def yperm(a):
        return lax.ppermute(a, "ctx", [(c, c ^ GROUP) for c in range(devices)])

    sent = call(
        functools.partial(prep_kernel, toks),
        [zpart] * GROUP + [part] * GROUP + [((1, glob), jnp.int32)],
        tuple(pltpu.with_memory_space_constraint(a, pltpu.HBM) for a in (positions.reshape(1, glob), queries, keys, values, grad_out)),
        scratch=[
            ((CAP, 2 * width), BF16),
            ((1, glob), jnp.int32),
            ((toks, width), BF16),
            ((toks, width), BF16),
            ((toks, kwidth), BF16),
            ((toks, kwidth), BF16),
        ],
        specs=[HBM] * 5,
        sems=5,
        moved=4 << 20,
    )
    pos = sent[2 * GROUP]
    zs = [sent[0]] + [zperm(sent[step], step) for step in range(1, GROUP)]
    kv0, qc = call(
        functools.partial(join_kernel, toks), [cpart, ((GROUP * PIECES * CAP + BLOCK, KV), BF16)], tuple(zs), moved=1 << 20
    )
    kvs = [kv0] + [xperm(kv0, m) for m in range(1, XS)]
    qcp = yperm(qc)
    qgs = [sent[GROUP]] + [zperm(sent[GROUP + step], step) for step in range(1, GROUP)]
    (e2,) = call(functools.partial(pick_kernel, ctoks), [ppart], (pos, *kvs), moved=6 << 20)
    e2p = yperm(e2)
    (st,) = call(
        functools.partial(stats_kernel, toks),
        [((glob // CHUNK, 8, GROWS), F32)],
        (pos, *kvs, qc, qcp),
        scratch=[((2 * GROUP * CAP, 2 * WIDE), BF16), ((XS * ctoks, GROWS), F32)],
        moved=14 << 20,
    )
    stp = yperm(st)
    *outs, dw, dkg, e5, edge = call(
        functools.partial(near_kernel, seq, toks),
        [part] * GROUP + [((ctoks, KV), F32), ((glob, KV), F32), ppart, ((BLOCK, KV), BF16)],
        (pos, st, kv0, e2, e2p, qcp, *qgs),
        scratch=[
            ((ctoks + 2 * BLOCK, KV), BF16),
            ((ctoks + 2 * BLOCK, KV), F32),
            ((glob, KV), BF16),
            ((KV, glob), BF16),
            ((ctoks, 2 * WIDE), BF16),
            ((ctoks, 2 * WIDE), BF16),
        ],
        moved=40 << 20,
    )
    e5p = yperm(e5)
    os = [outs[0]] + [zperm(outs[step], step) for step in range(1, GROUP)]
    dkv, e4, keep = call(
        functools.partial(grads_kernel, toks),
        [((XS, ctoks, KV), F32), ((GROUP * CAP + EDGE, 2 * WIDE), BF16), ((GROUP * CAP, 2 * WIDE), F32)],
        (pos, *kvs, qc, qcp, st, stp, dw, dkg, edge),
        scratch=[
            ((2 * GROUP * CAP, 2 * WIDE), BF16),
            ((XS, KV, ctoks), BF16),
            ((2 * GROUP * CAP, 2 * WIDE), F32),
        ],
        moved=24 << 20,
    )
    own, *sends = call(
        functools.partial(peer_kernel, toks),
        [((ctoks, KV), F32)] + [cpart] * (XS - 1),
        (pos, dkv, e5p),
        moved=3 << 20,
    )
    got = [xperm(sends[m - 1], m) for m in range(1, XS)]
    e4p = yperm(e4)
    zback = call(
        functools.partial(merge_kernel, toks),
        [zpart] * GROUP,
        (pos, own, *got, keep, e4p),
        scratch=[((ctoks, KV), BF16)],
        moved=3 << 20,
    )
    zr = [zback[0]] + [zperm(zback[step], step) for step in range(1, GROUP)]
    return call(
        functools.partial(post_kernel, toks),
        [((toks, width), BF16)] * 2 + [((toks, kwidth), BF16)] * 2,
        (pos, *zr, *os),
        moved=4 << 20,
    )


def solution(mesh):
    rows = P(("dp", "ctx"), None)
    return jax.shard_map(
        local,
        mesh=mesh,
        in_specs=(rows, rows, rows, rows, P("dp")),
        out_specs=(rows, rows, rows, rows),
        check_vma=False,
    )
```

```python
import functools
import math

import jax
import jax.numpy as jnp
from jax import lax
from jax.experimental import pallas as pl
from jax.experimental.pallas import tpu as pltpu
from jax.sharding import PartitionSpec as P


HQ = 16
HK = 4
DH = 128
BLOCK = 64
CAP = 32
REP = HQ // HK
GROUP = 4
SIDES = 2
XS = 4
CHUNK = 128
ROWS = REP * BLOCK
GROWS = REP * CHUNK
WIDE = REP * DH
KV = 2 * DH
PIECES = 2 * WIDE // KV
EDGE = BLOCK // PIECES
SCALE = 1.0 / math.sqrt(DH)
EXP2 = SCALE * math.log2(math.e)
NEG = -1e30

F32 = jnp.float32
BF16 = jnp.bfloat16


def dot_nt(a, b):
    return lax.dot_general(a, b, (((1,), (1,)), ((), ())), preferred_element_type=F32)


def dot_nn(a, b):
    return lax.dot_general(a, b, (((1,), (0,)), ((), ())), preferred_element_type=F32)


def iota(shape, dim):
    return lax.broadcasted_iota(jnp.int32, shape, dim)


def hot(mask):
    return mask.astype(F32).astype(BF16)


def split(x):
    high = x.astype(BF16)
    return high, (x - high.astype(F32)).astype(BF16)


def place():
    me = lax.axis_index("ctx")
    cluster = me // GROUP
    return me, cluster // SIDES, lax.rem(cluster, SIDES), lax.rem(me, GROUP)


def column(row):
    n = row.shape[1]
    eye = iota((n, n), 0) == iota((n, n), 1)
    wide = jnp.where(eye, jnp.broadcast_to(row, (n, n)), 0).astype(F32)
    return jnp.sum(wide, axis=1, keepdims=True).astype(jnp.int32)


def below(pos_row, edge):
    return jnp.sum((pos_row < edge).astype(F32), axis=1, keepdims=True).astype(jnp.int32)


def pair_count(pos_row, x, toks):
    size = SIDES * GROUP * toks
    inside = (pos_row >= x * size) & (pos_row < (x + 1) * size)
    return jnp.sum(inside.astype(F32)).astype(jnp.int32)


def slots_along_lanes(pos_col, tok_row, before):
    is_row = jnp.sum((pos_col == tok_row).astype(F32), axis=0, keepdims=True)
    rank = jnp.sum((pos_col < tok_row).astype(F32), axis=0, keepdims=True).astype(jnp.int32)
    return jnp.where(is_row > 0.5, rank - before, -1)


def slots_along_rows(pos_row, tok_col, before):
    is_col = jnp.sum((pos_row == tok_col).astype(F32), axis=1, keepdims=True)
    rank = jnp.sum((pos_row < tok_col).astype(F32), axis=1, keepdims=True).astype(jnp.int32)
    return jnp.where(is_col > 0.5, rank - before, -1)


def prep_kernel(toks, pos_any, q_any, k_any, v_any, g_any, *refs):
    zs_refs, qg_refs, pos_out = refs[:GROUP], refs[GROUP : 2 * GROUP], refs[2 * GROUP]
    picked, pos_ref, q_ref, g_ref, k_ref, v_ref, sems = refs[2 * GROUP + 1 :]
    pos_copy = pltpu.make_async_copy(pos_any, pos_ref, sems.at[4])
    pos_copy.start()
    copies = [
        pltpu.make_async_copy(src, dst, sems.at[i])
        for i, (src, dst) in enumerate(((q_any, q_ref), (g_any, g_ref), (k_any, k_ref), (v_any, v_ref)))
    ]
    for copy in copies:
        copy.start()
    me, _, _, z = place()
    pos_copy.wait()
    pos_row = pos_ref[...]
    pos_out[...] = pos_row
    first = me * toks
    slot = slots_along_lanes(column(pos_row), first + iota((1, toks), 1), below(pos_row, first))
    pick = hot(slot == iota((CAP, toks), 0))
    width = HQ * DH
    for copy in copies:
        copy.wait()
    picked[:, :width] = dot_nn(pick, q_ref[...]).astype(BF16)
    picked[:, width:] = dot_nn(pick, g_ref[...]).astype(BF16)
    for step in range(GROUP):
        j = lax.rem(z + step, GROUP)
        head = pl.ds(pl.multiple_of(j * DH, DH), DH)
        cols = pl.ds(pl.multiple_of(j * WIDE, WIDE), WIDE)
        zs_refs[step][:toks, :DH] = k_ref[:, head]
        zs_refs[step][:toks, DH:] = v_ref[:, head]
        for p in range(PIECES):
            base = j * WIDE + p * KV if p * KV < WIDE else width + j * WIDE + p * KV - WIDE
            part = picked[:, pl.ds(pl.multiple_of(base, KV), KV)]
            zs_refs[step][toks + CAP * p : toks + CAP * (p + 1), :] = part
        qg_refs[step][:, :WIDE] = q_ref[:, cols]
        qg_refs[step][:, WIDE:] = g_ref[:, cols]


def join_kernel(toks, *refs):
    zs_refs, kv_ref, qc_ref = refs[:GROUP], refs[GROUP], refs[GROUP + 1]
    _, _, y, z = place()
    for step in range(GROUP):
        src = lax.rem(z + GROUP - step, GROUP)
        kv_ref[pl.ds(pl.multiple_of(src * toks, toks), toks), :] = zs_refs[step][:toks, :]
        rows = PIECES * CAP
        qc_ref[pl.ds(pl.multiple_of(src * rows, rows), rows), :] = zs_refs[step][toks:, :]
    last = slice((GROUP * toks) - BLOCK, GROUP * toks)
    qc_ref[GROUP * PIECES * CAP :, :] = jnp.where(y == 0, kv_ref[last, :], kv_ref[:BLOCK, :])


def side_first(x, y, m, ctoks):
    return (lax.rem(x + XS - m, XS) * SIDES + y) * ctoks


def pick_kernel(ctoks, pos_ref, *refs):
    kv_refs, out_ref = refs[:XS], refs[XS]
    _, x, y, _ = place()
    pos_row = pos_ref[...]
    glob = pos_row.shape[1]
    pos_col = column(pos_row)
    got = jnp.zeros((glob, KV), F32)
    for m in range(XS):
        first = side_first(x, y, m, ctoks)
        got = got + dot_nn(hot(pos_col == first + iota((glob, ctoks), 1)), kv_refs[m][...])
    out_ref[:glob, :] = got.astype(BF16)
    end = slice(ctoks - BLOCK, ctoks)
    out_ref[glob:, :] = jnp.where(y == 0, kv_refs[3][:BLOCK, :], kv_refs[1][end, :])


def fill_slots(y, slots, mine_ref, peer_ref):
    half = GROUP * CAP
    rows = PIECES * CAP
    for ref, side in ((mine_ref, y), (peer_ref, 1 - y)):
        for d in range(GROUP):
            at = pl.ds(pl.multiple_of(side * half + d * CAP, CAP), CAP)
            for p in range(PIECES):
                begin = d * rows + p * CAP
                slots[at, p * KV : (p + 1) * KV] = ref[begin : begin + CAP, :]


def padded_ranks(x, toks, pos_col, before):
    lane = iota((1, 2 * GROUP * CAP), 1)
    dev = x * (SIDES * GROUP) + lane // CAP
    start = jnp.sum((pos_col < dev * toks).astype(F32), axis=0, keepdims=True).astype(jnp.int32)
    stop = jnp.sum((pos_col < (dev + 1) * toks).astype(F32), axis=0, keepdims=True).astype(jnp.int32)
    rank = start + lax.rem(lane, CAP)
    return jnp.where(rank < stop, rank - before, -1)


def chunk_rows(slots, ranks, base):
    pick = hot(ranks == base + iota((CHUNK, ranks.shape[1]), 0))
    got = dot_nn(pick, slots[...]).astype(BF16)
    q = jnp.concatenate([got[:, h * DH : (h + 1) * DH] for h in range(REP)], axis=0)
    g = jnp.concatenate([got[:, WIDE + h * DH : WIDE + (h + 1) * DH] for h in range(REP)], axis=0)
    return q, g


def stats_kernel(toks, pos_ref, *refs):
    kv_refs, mine_ref, peer_ref, out_ref = refs[:XS], refs[XS], refs[XS + 1], refs[XS + 2]
    slots, sc = refs[XS + 3 :]
    _, x, y, _ = place()
    pos_row = pos_ref[...]
    before = below(pos_row, x * (SIDES * GROUP * toks))
    fill_slots(y, slots, mine_ref, peer_ref)
    ranks = padded_ranks(x, toks, column(pos_row), before)
    ctoks = GROUP * toks
    out_ref[...] = jnp.zeros_like(out_ref)

    def chunk(ch, carry):
        q, g = chunk_rows(slots, ranks, ch * CHUNK)
        top = jnp.full((1, GROWS), NEG, F32)
        for m in range(XS):
            s = dot_nt(kv_refs[m][:, :DH], q)
            sc[m * ctoks : (m + 1) * ctoks, :] = s
            top = jnp.maximum(top, jnp.max(s, axis=0, keepdims=True))
        total = jnp.zeros((1, GROWS), F32)
        dsum = jnp.zeros((1, GROWS), F32)
        for m in range(XS):
            w = jnp.exp2((sc[m * ctoks : (m + 1) * ctoks, :] - top) * EXP2)
            total = total + jnp.sum(w, axis=0, keepdims=True)
            dsum = dsum + jnp.sum(w * dot_nt(kv_refs[m][:, DH:], g), axis=0, keepdims=True)
        out_ref[ch, 0:1, :] = top
        out_ref[ch, 1:2, :] = total
        out_ref[ch, 2:3, :] = dsum
        return carry

    lax.fori_loop(0, (pair_count(pos_row, x, toks) + CHUNK - 1) // CHUNK, chunk, 0)


def near_kernel(seq, toks, pos_ref, after_ref, kv_ref, e2_ref, e2p_ref, qcp_ref, *refs):
    qg_in = refs[:GROUP]
    outs = refs[GROUP : 2 * GROUP]
    dw_ref, dkg_ref, e5_ref, edge_ref, win, dwin, kg, kgt, qg, out = refs[2 * GROUP :]
    me, _, y, z = place()
    ctoks = GROUP * toks
    pos_row = pos_ref[...]
    glob = pos_row.shape[1]
    pos_col = column(pos_row)
    first = (me // GROUP) * ctoks
    far_edge = e2p_ref[glob:, :]
    near_edge = qcp_ref[GROUP * PIECES * CAP :, :]
    win[:BLOCK, :] = jnp.where(y == 0, far_edge, near_edge)
    win[BLOCK : BLOCK + ctoks, :] = kv_ref[...]
    win[BLOCK + ctoks :, :] = jnp.where(y == 0, near_edge, far_edge)
    both = (e2_ref[:glob, :].astype(F32) + e2p_ref[:glob, :].astype(F32)).astype(BF16)
    kg[...] = both
    kgt[...] = both.T
    for step in range(GROUP):
        src = lax.rem(z + GROUP - step, GROUP)
        qg[pl.ds(pl.multiple_of(src * toks, toks), toks), :] = qg_in[step][...]
    dwin[...] = jnp.zeros_like(dwin)
    dkg_ref[...] = jnp.zeros_like(dkg_ref)

    def block(b, carry):
        base = first + b * BLOCK
        here = pl.ds(pl.multiple_of(b * BLOCK, BLOCK), 3 * BLOCK)
        mine = pl.ds(pl.multiple_of(b * BLOCK, BLOCK), BLOCK)
        kn, vn = win[here, :DH], win[here, DH:]
        q = jnp.concatenate([qg[mine, h * DH : (h + 1) * DH] for h in range(REP)], axis=0)
        g = jnp.concatenate([qg[mine, WIDE + h * DH : WIDE + (h + 1) * DH] for h in range(REP)], axis=0)
        key_tok = base - BLOCK + iota((3 * BLOCK, 1), 0)
        key_glob = jnp.sum((key_tok == pos_row).astype(F32), axis=1, keepdims=True)
        usable = (key_tok >= 0) & (key_tok < seq) & (key_glob < 0.5)
        row_tok = base + lax.rem(iota((1, ROWS), 1), BLOCK)
        live = 1.0 - jnp.sum((pos_col == row_tok).astype(F32), axis=0, keepdims=True)

        sn = jnp.where(usable, dot_nt(kn, q), NEG)
        sf = dot_nt(kg[:, :DH], q)
        top = jnp.maximum(jnp.max(sn, axis=0, keepdims=True), jnp.max(sf, axis=0, keepdims=True))
        wn = jnp.exp2((sn - top) * EXP2)
        wf = jnp.exp2((sf - top) * EXP2)
        dn = dot_nt(vn, g)
        df = dot_nt(kg[:, DH:], g)
        total = jnp.sum(wn, axis=0, keepdims=True) + jnp.sum(wf, axis=0, keepdims=True)
        dsum = jnp.sum(wn * dn, axis=0, keepdims=True) + jnp.sum(wf * df, axis=0, keepdims=True)
        inv = 1.0 / total
        delta = dsum * inv
        mixed = (dot_nn(vn.T, wn.astype(BF16)) + dot_nn(kgt[DH:, :], wf.astype(BF16))) * inv
        inv_live = inv * live
        pn = wn * inv_live
        pf = wf * inv_live
        dsn = (pn * (dn - delta)).astype(BF16)
        dsf = (pf * (df - delta)).astype(BF16)
        gq = (dot_nn(kn.T, dsn) + dot_nn(kgt[:DH, :], dsf)) * SCALE
        dwin[here, :DH] += dot_nn(dsn, q) * SCALE
        dwin[here, DH:] += dot_nn(pn.astype(BF16), g)
        dkg_ref[:, :DH] += dot_nn(dsf, q) * SCALE
        dkg_ref[:, DH:] += dot_nn(pf.astype(BF16), g)
        att = mixed.T.astype(BF16)
        gqr = gq.T.astype(BF16)
        for h in range(REP):
            rows = slice(h * BLOCK, (h + 1) * BLOCK)
            out[mine, h * DH : (h + 1) * DH] = att[rows]
            out[mine, WIDE + h * DH : WIDE + (h + 1) * DH] = gqr[rows]
        return carry

    lax.fori_loop(0, ctoks // BLOCK, block, 0, unroll=4)
    for step in range(GROUP):
        dst = lax.rem(z + step, GROUP)
        outs[step][...] = out[pl.ds(pl.multiple_of(dst * toks, toks), toks), :]
    dw_ref[...] = dwin[BLOCK : BLOCK + ctoks, :]
    e5_ref[:glob, :] = dkg_ref[...].astype(BF16)
    low, high = dwin[:BLOCK, :], dwin[BLOCK + ctoks :, :]
    e5_ref[glob:, :] = jnp.where(y == 0, low, high).astype(BF16)
    edge_ref[...] = jnp.where(y == 0, high, low).astype(BF16)


def grads_kernel(toks, pos_ref, *refs):
    kv_refs, refs = refs[:XS], refs[XS:]
    mine_ref, peer_ref, st_ref, stp_ref, dw_ref, edge_ref = refs[:6]
    dkv, e4_ref, keep_ref, slots, kvt, rows_out = refs[6:]
    _, x, y, _ = place()
    ctoks = GROUP * toks
    pos_row = pos_ref[...]
    pos_col = column(pos_row)
    pair_first = x * (SIDES * ctoks)
    before = below(pos_row, pair_first)
    count = pair_count(pos_row, x, toks)
    fill_slots(y, slots, mine_ref, peer_ref)
    ranks = padded_ranks(x, toks, pos_col, before)
    rows_out[...] = jnp.zeros_like(rows_out)
    for m in range(XS):
        kvt[m] = kv_refs[m][...].T

    dkv[0] = dw_ref[...]
    for m in range(1, XS):
        dkv[m] = jnp.zeros((ctoks, KV), F32)

    def chunk(ch, carry):
        base = ch * CHUNK
        q, g = chunk_rows(slots, ranks, base)
        valid = (base + lax.rem(iota((1, GROWS), 1), CHUNK) < count).astype(F32)
        here, there = st_ref[ch], stp_ref[ch]
        top = jnp.maximum(here[0:1], there[0:1])
        a = jnp.exp2((here[0:1] - top) * EXP2)
        b = jnp.exp2((there[0:1] - top) * EXP2)
        inv = 1.0 / (here[1:2] * a + there[1:2] * b)
        delta = (here[2:3] * a + there[2:3] * b) * inv
        inv = inv * valid
        att = jnp.zeros((DH, GROWS), F32)
        gq = jnp.zeros((DH, GROWS), F32)
        for m in range(XS):
            p = jnp.exp2((dot_nt(kv_refs[m][:, :DH], q) - top) * EXP2) * inv
            p_high, p_low = split(p)
            ds = (p * (dot_nt(kv_refs[m][:, DH:], g) - delta)).astype(BF16)
            dkv[m, :, :DH] += dot_nn(ds, q) * SCALE
            dkv[m, :, DH:] += dot_nn(p_high, g)
            vt = kvt[m, DH:, :]
            att = att + dot_nn(vt, p_high) + dot_nn(vt, p_low)
            gq = gq + dot_nn(kvt[m, :DH, :], ds)
        att = att.T
        gq = (gq * SCALE).T
        rows = pl.ds(pl.multiple_of(base, CHUNK), CHUNK)
        for h in range(REP):
            part = slice(h * CHUNK, (h + 1) * CHUNK)
            rows_out[rows, h * DH : (h + 1) * DH] = att[part]
            rows_out[rows, WIDE + h * DH : WIDE + (h + 1) * DH] = gq[part]
        return carry

    lax.fori_loop(0, (count + CHUNK - 1) // CHUNK, chunk, 0)
    part_high, part_low = split(rows_out[...])
    slot = iota((GROUP * CAP, 2 * GROUP * CAP), 0)
    lane = iota((GROUP * CAP, 2 * GROUP * CAP), 1)

    def cluster_mask(side):
        begin = below(pos_row, pair_first + side * ctoks) - before
        size = below(pos_row, pair_first + (side + 1) * ctoks) - before - begin
        return hot((lane == begin + slot) & (slot < size))

    half = GROUP * CAP
    e4_ref[:half, :] = dot_nn(cluster_mask(1 - y), part_high).astype(BF16)
    for p in range(PIECES):
        e4_ref[half:, p * KV : (p + 1) * KV] = edge_ref[p * EDGE : (p + 1) * EDGE, :]
    mask = cluster_mask(y)
    keep_ref[...] = dot_nn(mask, part_high) + dot_nn(mask, part_low)


def peer_kernel(toks, pos_ref, dkv_ref, dkg_ref, e5p_ref, own_ref, *send_refs):
    _, x, y, _ = place()
    ctoks = GROUP * toks
    pos_row = pos_ref[...]
    glob = pos_row.shape[1]
    far_high, far_low = split(dkg_ref[...] + e5p_ref[:glob, :].astype(F32))
    edge = e5p_ref[glob:, :].astype(F32)
    at_zero = (y == 0).astype(F32)
    at_one = 1.0 - at_zero
    none = jnp.zeros((ctoks - BLOCK, KV), F32)
    edges = {
        1: jnp.concatenate([none, edge * at_one], axis=0),
        3: jnp.concatenate([edge * at_zero, none], axis=0),
    }
    for m in range(XS):
        first = side_first(x, y, m, ctoks)
        mask = hot(first + iota((ctoks, glob), 0) == pos_row)
        whole = dkv_ref[m] + dot_nn(mask, far_high) + dot_nn(mask, far_low)
        if m in edges:
            whole = whole + edges[m]
        if m == 0:
            own_ref[...] = whole
        else:
            send_refs[XS - m - 1][...] = whole.astype(BF16)


def merge_kernel(toks, pos_ref, own_ref, *refs):
    got_refs, refs = refs[: XS - 1], refs[XS - 1 :]
    keep_ref, e4p_ref = refs[0], refs[1]
    zs_refs, whole = refs[2 : 2 + GROUP], refs[2 + GROUP]
    me, _, y, z = place()
    pos_row = pos_ref[...]
    total = own_ref[...]
    for ref in got_refs:
        total = total + ref[...].astype(F32)
    half = GROUP * CAP
    edge = [e4p_ref[half:, p * KV : (p + 1) * KV] for p in range(PIECES)]
    edge = jnp.concatenate(edge, axis=0).astype(F32)
    at_zero = (y == 0).astype(F32)
    none = jnp.zeros((GROUP * toks - 2 * BLOCK, KV), F32)
    total = total + jnp.concatenate([edge * (1.0 - at_zero), none, edge * at_zero], axis=0)
    whole[...] = total.astype(BF16)
    rows = (keep_ref[...] + e4p_ref[:half, :].astype(F32)).astype(BF16)
    first_dev = (me // GROUP) * GROUP
    before = below(pos_row, first_dev * toks)
    slot = iota((CAP, GROUP * CAP), 0)
    lane = iota((CAP, GROUP * CAP), 1)
    for step in range(GROUP):
        j = lax.rem(z + step, GROUP)
        zs_refs[step][:toks, :] = whole[pl.ds(pl.multiple_of(j * toks, toks), toks), :]
        begin = below(pos_row, (first_dev + j) * toks) - before
        size = below(pos_row, (first_dev + j + 1) * toks) - before - begin
        got = dot_nn(hot((lane == begin + slot) & (slot < size)), rows).astype(BF16)
        for p in range(PIECES):
            zs_refs[step][toks + CAP * p : toks + CAP * (p + 1), :] = got[:, p * KV : (p + 1) * KV]


def post_kernel(toks, pos_ref, *refs):
    zs_refs, o_refs = refs[:GROUP], refs[GROUP : 2 * GROUP]
    att_ref, gq_ref, dk_ref, dv_ref = refs[2 * GROUP :]
    me, _, _, z = place()
    pos_row = pos_ref[...]
    first = me * toks
    slot = slots_along_rows(pos_row, first + iota((toks, 1), 0), below(pos_row, first))
    mask = hot(slot == iota((toks, CAP), 1))
    is_glob = slot >= 0
    for step in range(GROUP):
        j = lax.rem(z + GROUP - step, GROUP)
        head = pl.ds(pl.multiple_of(j * DH, DH), DH)
        dk_ref[:, head] = zs_refs[step][:toks, :DH]
        dv_ref[:, head] = zs_refs[step][:toks, DH:]
        for p in range(PIECES):
            rows = zs_refs[step][toks + CAP * p : toks + CAP * (p + 1), :]
            placed = dot_nn(mask, rows)
            here = o_refs[step][:, p * KV : (p + 1) * KV].astype(F32)
            value = jnp.where(is_glob, placed, here).astype(BF16)
            ref, off = (att_ref, p * KV) if p * KV < WIDE else (gq_ref, p * KV - WIDE)
            ref[:, pl.ds(pl.multiple_of(j * WIDE + off, KV), KV)] = value


VM = pl.BlockSpec(memory_space=pltpu.VMEM)
HBM = pl.BlockSpec(memory_space=pltpu.HBM)


def call(kernel, outs, args, scratch=(), specs=None, sems=0, flops=0, moved=0):
    return pl.pallas_call(
        kernel,
        out_shape=tuple(jax.ShapeDtypeStruct(s, d) for s, d in outs),
        in_specs=specs or [VM] * len(args),
        out_specs=(VM,) * len(outs),
        scratch_shapes=[pltpu.VMEM(s, d) for s, d in scratch] + [pltpu.SemaphoreType.DMA((sems,))] * (sems > 0),
        compiler_params=pltpu.CompilerParams(vmem_limit_bytes=40 * 1024 * 1024),
        cost_estimate=pl.CostEstimate(flops=flops, bytes_accessed=moved, transcendentals=0),
    )(*args)


def local(queries, keys, values, grad_out, positions):
    toks, width = queries.shape
    kwidth = keys.shape[1]
    devices = lax.axis_size("ctx")
    seq = toks * devices
    ctoks = GROUP * toks
    glob = positions.shape[0]
    zrows = toks + PIECES * CAP
    part = ((toks, 2 * WIDE), BF16)
    zpart = ((zrows, KV), BF16)
    cpart = ((ctoks, KV), BF16)
    ppart = ((glob + BLOCK, KV), BF16)

    def zperm(a, step):
        pairs = [(c, c // GROUP * GROUP + (c + step) % GROUP) for c in range(devices)]
        return lax.ppermute(a, "ctx", pairs)

    def xperm(a, step):
        return lax.ppermute(a, "ctx", [(c, (c + step * SIDES * GROUP) % devices) for c in range(devices)])

    def yperm(a):
        return lax.ppermute(a, "ctx", [(c, c ^ GROUP) for c in range(devices)])

    sent = call(
        functools.partial(prep_kernel, toks),
        [zpart] * GROUP + [part] * GROUP + [((1, glob), jnp.int32)],
        tuple(pltpu.with_memory_space_constraint(a, pltpu.HBM) for a in (positions.reshape(1, glob), queries, keys, values, grad_out)),
        scratch=[
            ((CAP, 2 * width), BF16),
            ((1, glob), jnp.int32),
            ((toks, width), BF16),
            ((toks, width), BF16),
            ((toks, kwidth), BF16),
            ((toks, kwidth), BF16),
        ],
        specs=[HBM] * 5,
        sems=5,
        moved=4 << 20,
    )
    pos = sent[2 * GROUP]
    zs = [sent[0]] + [zperm(sent[step], step) for step in range(1, GROUP)]
    kv0, qc = call(
        functools.partial(join_kernel, toks), [cpart, ((GROUP * PIECES * CAP + BLOCK, KV), BF16)], tuple(zs), moved=1 << 20
    )
    kvs = [kv0] + [xperm(kv0, m) for m in range(1, XS)]
    qcp = yperm(qc)
    qgs = [sent[GROUP]] + [zperm(sent[GROUP + step], step) for step in range(1, GROUP)]
    (e2,) = call(functools.partial(pick_kernel, ctoks), [ppart], (pos, *kvs), moved=6 << 20)
    e2p = yperm(e2)
    (st,) = call(
        functools.partial(stats_kernel, toks),
        [((glob // CHUNK, 8, GROWS), F32)],
        (pos, *kvs, qc, qcp),
        scratch=[((2 * GROUP * CAP, 2 * WIDE), BF16), ((XS * ctoks, GROWS), F32)],
        moved=14 << 20,
    )
    stp = yperm(st)
    *outs, dw, dkg, e5, edge = call(
        functools.partial(near_kernel, seq, toks),
        [part] * GROUP + [((ctoks, KV), F32), ((glob, KV), F32), ppart, ((BLOCK, KV), BF16)],
        (pos, st, kv0, e2, e2p, qcp, *qgs),
        scratch=[
            ((ctoks + 2 * BLOCK, KV), BF16),
            ((ctoks + 2 * BLOCK, KV), F32),
            ((glob, KV), BF16),
            ((KV, glob), BF16),
            ((ctoks, 2 * WIDE), BF16),
            ((ctoks, 2 * WIDE), BF16),
        ],
        moved=40 << 20,
    )
    e5p = yperm(e5)
    os = [outs[0]] + [zperm(outs[step], step) for step in range(1, GROUP)]
    dkv, e4, keep = call(
        functools.partial(grads_kernel, toks),
        [((XS, ctoks, KV), F32), ((GROUP * CAP + EDGE, 2 * WIDE), BF16), ((GROUP * CAP, 2 * WIDE), F32)],
        (pos, *kvs, qc, qcp, st, stp, dw, edge),
        scratch=[
            ((2 * GROUP * CAP, 2 * WIDE), BF16),
            ((XS, KV, ctoks), BF16),
            ((2 * GROUP * CAP, 2 * WIDE), F32),
        ],
        moved=24 << 20,
    )
    own, *sends = call(
        functools.partial(peer_kernel, toks),
        [((ctoks, KV), F32)] + [cpart] * (XS - 1),
        (pos, dkv, dkg, e5p),
        moved=3 << 20,
    )
    got = [xperm(sends[m - 1], m) for m in range(1, XS)]
    e4p = yperm(e4)
    zback = call(
        functools.partial(merge_kernel, toks),
        [zpart] * GROUP,
        (pos, own, *got, keep, e4p),
        scratch=[((ctoks, KV), BF16)],
        moved=3 << 20,
    )
    zr = [zback[0]] + [zperm(zback[step], step) for step in range(1, GROUP)]
    return call(
        functools.partial(post_kernel, toks),
        [((toks, width), BF16)] * 2 + [((toks, kwidth), BF16)] * 2,
        (pos, *zr, *os),
        moved=4 << 20,
    )


def solution(mesh):
    rows = P(("dp", "ctx"), None)
    return jax.shard_map(
        local,
        mesh=mesh,
        in_specs=(rows, rows, rows, rows, P("dp")),
        out_specs=(rows, rows, rows, rows),
        check_vma=False,
    )
```
